32 devices in a mesh: conf: 2 (over x), virt: 16 (over z, y, core).
Axes of the slice: x: 2, y: 2, z: 4, core: 2. Of those that a mesh axis runs over, the one named last changes fastest.
Arguments:
- i_factors: float32 [32, 1024, 2048], P('conf', 'virt'), parts along dimension 0, may hold values from -0.6 to 0.6
- j_factors: float32 [4, 1024, 2048], P('conf', 'virt'), parts along dimension 0, may hold values from -0.6 to 0.6
- occ_i: float32 [32], P('conf'), parts along dimension 0, may hold values from -2 to -0.3
- occ_j: float32 [4], P('conf'), parts along dimension 0, may hold values from -2 to -0.3
- virt_energy: float32 [2048], P(('conf', 'virt')), parts along dimension 0, may hold values from 0.3 to 3
Outputs:
- density: float32 [32, 1024, 2048], P('conf', 'virt'), parts along dimension 0
The draws below stay inside these ranges and needn't reach their ends.
There are 2 independent parts, one for each index of `conf`. The reference program is written for one: setup_inputs(seed, part) draws one part's arguments, and reference() takes and returns one part's arrays. A program takes and returns all parts, laid end to end along the dimension named above; each array names one. Nothing has to cross between parts.
All inputs are finite; a program needn't handle non-finite values.
Results may differ from the reference program's by a relative error of at most 0.00005.
Values sent between devices are 32-bit elements; how exact they have to be, the bound alone decides.
A program may use at most 128 MiB of HBM per device.

```python
import jax
import jax.numpy as jnp
from jax import lax

NV = 1024
NAUX = 2048
NJ = 2
NI = 16


def level_of(own_key, extent, pieces, least, top_value):
    loudness, own = 1.0, jax.random.fold_in(own_key, 6)
    for dim, blocks in pieces:
        steps = jnp.exp(jax.random.uniform(jax.random.fold_in(own, dim), (blocks,), jnp.float32, least / len(pieces), top_value / len(pieces)))
        loudness = loudness * jnp.repeat(steps, extent[dim] // blocks).reshape([-1 if axis == dim else 1 for axis in range(len(extent))])
    return loudness


def noise(stream_key, shape, spread, most, split=(), kind=jnp.bfloat16):
    array = jax.random.normal(stream_key, shape, jnp.float32) * spread
    if len(split) > 0:
        array = level_of(stream_key, shape, split, -0.22, 0.18) * array
    return jnp.clip(array, min=-most, max=most).astype(kind)


def setup_inputs(seed: int = 0, part: int = 0) -> dict:
    seeds = jax.random.split(jax.random.key(seed), 6)
    own_keys = jax.random.split(jax.random.fold_in(seeds[5], part), 6)
    return {
        "i_factors": noise(own_keys[0], (NI, NV, NAUX), 0.09, 0.6, ((1, 16),), jnp.float32),
        "j_factors": noise(own_keys[1], (NJ, NV, NAUX), 0.09, 0.6, ((1, 16),), jnp.float32),
        "occ_i": jnp.clip(jax.random.uniform(own_keys[2], (NI,), jnp.float32, -2.0, -0.3), -2.0, -0.3),
        "occ_j": jnp.clip(jax.random.uniform(own_keys[3], (NJ,), jnp.float32, -2.0, -0.3), -2.0, -0.3),
        "virt_energy": jnp.clip(0.3 + 2.7 * jax.random.uniform(own_keys[4], (NV,), jnp.float32) ** level_of(own_keys[4], (NV,), ((0, 16),), -0.2, 0.2), 0.3, 3.0),
    }


def reference(i_factors, j_factors, occ_i, occ_j, virt_energy):
    pair = jnp.einsum("iap,jbp->ijab", i_factors, j_factors, precision=lax.Precision.HIGHEST)
    swapped = jnp.swapaxes(pair, 2, 3)
    denominator = (virt_energy[None, None, :, None] + virt_energy[None, None, None, :]
                   - occ_i[:, None, None, None] - occ_j[None, :, None, None])
    amplitude = (swapped - 2.0 * pair) / denominator
    return jnp.einsum("ijab,jbp->iap", amplitude, j_factors, precision=lax.Precision.HIGHEST)
```

```python
import functools

import jax
import jax.numpy as jnp
from jax import lax
from jax.experimental import pallas as pl
from jax.experimental.pallas import tpu as pltpu
from jax.sharding import PartitionSpec as P

LANES = 128
MESH = pl.DeviceIdType.MESH


def split(value):
    high = value.astype(jnp.bfloat16)
    low = (value - high.astype(jnp.float32)).astype(jnp.bfloat16)
    return high, low


def kernel(
    n, columns, i_ref, j_ref, energy_ref, occ_i_ref, occ_j_ref, total,
    i_high, i_low, j_all, direct, x_send, x_recv, j_parts, amp_parts, row_ref,
    local_sem, j_send_sem, j_recv_sem, x_send_sem, x_recv_sem,
):
    levels = n // 2 // columns
    me = lax.axis_index("virt")
    core = lax.rem(me, 2)
    chip = me // 2
    y = lax.rem(chip, columns)
    z = chip // columns
    rows, depth = i_ref.shape
    pair = 2 * LANES
    tall = 256
    chunks = rows // tall

    load_i = pltpu.make_async_copy(i_ref, total, local_sem.at[0])
    load_i.start()
    load_j = pltpu.make_async_copy(j_ref, j_all.at[me], local_sem.at[1])
    load_j.start()

    barrier = pltpu.get_barrier_semaphore()

    def greet(device):
        pl.semaphore_signal(barrier, inc=1, device_id={"virt": device}, device_id_type=MESH)

    greet(me + 1 - 2 * core)
    if columns == 2:
        greet(me + 2 * (1 - 2 * y))

    @pl.when(z + 1 < levels)
    def _():
        greet(me + 2 * columns)

    @pl.when(z > 0)
    def _():
        greet(me - 2 * columns)

    inner = jnp.logical_and(z > 0, z + 1 < levels).astype(jnp.int32)
    pl.semaphore_wait(barrier, columns + (inner + 1 if levels > 1 else 0))

    def j_copy(origin, way, device):
        return pltpu.make_async_remote_copy(
            src_ref=j_all.at[origin],
            dst_ref=j_all.at[origin],
            send_sem=j_send_sem.at[origin, way],
            recv_sem=j_recv_sem.at[origin],
            device_id={"virt": device},
            device_id_type=MESH,
        )

    def j_targets(origin, act):
        place = origin // 2
        same_core = lax.rem(origin, 2) == core
        in_column = jnp.logical_and(same_core, lax.rem(place, columns) == y)
        from_z = place // columns

        @pl.when(jnp.logical_and(in_column, jnp.logical_and(z >= from_z, z + 1 < levels)))
        def _():
            act(j_copy(origin, 0, me + 2 * columns))

        @pl.when(jnp.logical_and(in_column, jnp.logical_and(z <= from_z, z > 0)))
        def _():
            act(j_copy(origin, 1, me - 2 * columns))

        if columns == 2:
            @pl.when(in_column)
            def _():
                act(j_copy(origin, 2, me + 2 * (1 - 2 * y)))

        @pl.when(same_core)
        def _():
            act(j_copy(origin, 3, me + 1 - 2 * core))

    def x_rows(chunk):
        return pl.ds(pl.multiple_of(chunk * tall, tall), tall)

    def x_copy(other, origin, part, slot):
        return pltpu.make_async_remote_copy(
            src_ref=x_send.at[other, part],
            dst_ref=x_recv.at[origin, part],
            send_sem=x_send_sem.at[other, slot],
            recv_sem=x_recv_sem.at[origin, slot],
            device_id={"virt": other},
            device_id_type=MESH,
        )

    def x_block(other, origin, chunk):
        return x_copy(other, origin, x_rows(chunk), chunk)

    def x_energy(other, origin):
        return x_copy(other, origin, pl.ds(rows, 1), chunks)

    def x_stay():
        return pltpu.make_async_copy(x_send.at[me], x_recv.at[me], local_sem.at[2])

    load_j.wait()
    j_targets(me, lambda copy: copy.start())
    load_i.wait()

    @pl.loop(0, rows // 32)
    def _(step):
        part = pl.ds(pl.multiple_of(step * 32, 32), 32)
        high, low = split(total[part, :])
        i_high[part, :] = high
        i_low[part, :] = low
        total[part, :] = jnp.zeros((32, depth), jnp.float32)

    width = energy_ref.shape[1]
    energy = energy_ref[...]
    twice = jnp.concatenate([energy, energy], axis=1)
    tall_energy = jnp.broadcast_to(twice, (LANES, LANES)).T[:width]
    for orbital in range(rows // width):
        row_ref[orbital * width:(orbital + 1) * width, :] = tall_energy - occ_i_ref[orbital]
    col_lane = lax.broadcasted_iota(jnp.int32, (8, LANES), 1)
    col_term = jnp.broadcast_to(twice, (8, LANES)) - jnp.where(
        col_lane < width, occ_j_ref[0], occ_j_ref[1]
    )

    @pl.loop(0, n)
    def _(other):
        x_send[other, pl.ds(rows, 8), :] = col_term

    def split_j(place, copies):
        per = LANES // 32

        @pl.loop(0, 2 * per)
        def _(step):
            from_rows = pl.ds(pl.multiple_of(lax.rem(step, per) * 32, 32), 32)
            high, low = split(j_all[2 * place + step // per, from_rows, :])
            base = pl.multiple_of(step * 32, 32)
            j_parts[pl.ds(base, 32), :] = high
            j_parts[pl.ds(pair + base, 32), :] = low
            if copies == 3:
                j_parts[pl.ds(2 * pair + base, 32), :] = high

    toward = jnp.where(2 * z >= levels, -1, 1)

    def visit(step):
        level = step // 4
        kind = lax.rem(step // 2, 2)
        sign = lax.rem(step, 2)
        distance = level - kind
        at_y = jnp.where(kind == 0, y, columns - 1 - y)

        def on(way):
            at_z = z + toward * (1 - 2 * way) * distance
            valid = jnp.logical_and(distance >= 0, jnp.logical_and(at_z >= 0, at_z < levels))
            valid = jnp.logical_and(valid, jnp.logical_or(distance > 0, way == 0))
            if columns == 1:
                valid = jnp.logical_and(valid, kind == 0)
            return valid, at_z * columns + at_y

        return on, sign

    visits = 4 * (levels + columns - 1)

    @pl.loop(0, visits)
    def _(step):
        on, sign = visit(step)

        @pl.when(sign == 0)
        def _():
            for way in range(2):
                valid, place = on(way)
                origin = 2 * place + core

                @pl.when(jnp.logical_and(valid, origin != me))
                def _():
                    j_copy(origin, 0, me).wait_recv()
                    j_targets(origin, lambda copy: copy.start())

        valid, place = on(sign)

        @pl.when(valid)
        def _():
            j_copy(2 * place + 1 - core, 0, me).wait_recv()
            for side in range(2):
                other = 2 * place + side

                @pl.when(other != me)
                def _():
                    x_energy(other, me).start()

            split_j(place, 2)
            lane = lax.broadcasted_iota(jnp.int32, (LANES // 2, LANES), 1)
            half = LANES // 2
            contract = (((1,), (1,)), ((), ()))

            @pl.loop(0, rows // tall)
            def _(block):
                start = pl.multiple_of(block * tall, tall)
                high, low = i_high[pl.ds(start, tall), :], i_low[pl.ds(start, tall), :]
                j_high, j_low = j_parts[pl.ds(0, pair), :], j_parts[pl.ds(pair, pair), :]
                dot = functools.partial(
                    lax.dot_general, dimension_numbers=contract,
                    preferred_element_type=jnp.float32,
                )
                block_pair = dot(high, j_high) + (dot(high, j_low) + dot(low, j_high))
                direct[place, pl.ds(start, tall), :] = block_pair
                for side in range(2):
                    for group in range(tall // LANES):
                        tile = block_pair[
                            group * LANES:(group + 1) * LANES, side * LANES:(side + 1) * LANES
                        ]
                        turned = tile.T
                        moved = pltpu.roll(turned, half, 1)
                        first = jnp.where(lane < half, turned[:half], moved[half:])
                        second = jnp.where(lane < half, moved[:half], turned[half:])
                        base = start + group * LANES
                        x_send[2 * place + side, pl.ds(base, half), :] = first
                        x_send[2 * place + side, pl.ds(base + half, half), :] = second
                for side in range(2):
                    other = 2 * place + side

                    @pl.when(other != me)
                    def _():
                        x_block(other, me, block).start()

            for side in range(2):
                other = 2 * place + side

                @pl.when(other == me)
                def _():
                    x_stay().start()

    def await_energies(place):
        for side in range(2):
            other = 2 * place + side

            @pl.when(other != me)
            def _():
                x_energy(other, other).wait_recv()

            @pl.when(other == me)
            def _():
                x_stay().wait()

    def await_blocks(place, chunk):
        for side in range(2):
            other = 2 * place + side

            @pl.when(other != me)
            def _():
                x_block(other, other, chunk).wait_recv()

    def amplitudes(place, part):
        for side in range(2):
            other = 2 * place + side
            lanes = slice(side * LANES, (side + 1) * LANES)
            swapped = x_recv[other, part, :]
            own = direct[place, part, lanes]
            denominator = row_ref[part, :] + x_recv[other, pl.ds(rows, 1), :]
            high, low = split((swapped - 2.0 * own) / denominator)
            amp_parts[part, side * LANES:(side + 1) * LANES] = high
            amp_parts[part, pair + side * LANES:pair + (side + 1) * LANES] = high
            amp_parts[part, 2 * pair + side * LANES:2 * pair + (side + 1) * LANES] = low

    farthest = jnp.maximum(z, levels - 1 - z)
    if columns == 2 and levels > 1:
        farthest = jnp.where(farthest == levels - 1, farthest - 1, farthest)
    back = z - toward * farthest
    forth = z + toward * farthest
    back_valid = jnp.logical_and(back >= 0, back < levels)
    last_place = jnp.where(back_valid, back, forth) * columns + columns - 1 - y

    @pl.loop(0, visits)
    def _(step):
        on, sign = visit(step)
        valid, place = on(sign)

        @pl.when(jnp.logical_and(valid, place != last_place))
        def _():
            split_j(place, 3)
            await_energies(place)

            @pl.loop(0, chunks)
            def _(block):
                await_blocks(place, block)
                amplitudes(place, x_rows(block))

            @pl.loop(0, depth // pair)
            def _(strip):
                at = pl.ds(pl.multiple_of(strip * pair, pair), pair)
                total[:, at] += jnp.dot(
                    amp_parts[...], j_parts[:, at], preferred_element_type=jnp.float32
                )

    split_j(last_place, 3)

    @pl.loop(0, n)
    def _(other):
        j_targets(other, lambda copy: copy.wait_send())

    await_energies(last_place)

    @pl.loop(0, chunks)
    def _(block):
        part = x_rows(block)
        await_blocks(last_place, block)
        amplitudes(last_place, part)

        @pl.loop(0, depth // pair)
        def _(strip):
            at = pl.ds(pl.multiple_of(strip * pair, pair), pair)
            total[part, at] += jnp.dot(
                amp_parts[part, :], j_parts[:, at], preferred_element_type=jnp.float32
            )

    @pl.loop(0, n)
    def _(other):
        @pl.when(other != me)
        def _():
            x_energy(other, me).wait_send()

            @pl.loop(0, chunks)
            def _(chunk):
                x_block(other, me, chunk).wait_send()


def fused(columns, i_factors, j_factors, occ_i, occ_j, virt_energy):
    n = lax.axis_size("virt")
    ni, width, depth = i_factors.shape
    nj = j_factors.shape[0]
    rows = ni * width
    anywhere = pl.BlockSpec(memory_space=pl.ANY)
    vmem = pl.BlockSpec(memory_space=pltpu.VMEM)
    f32, bf16 = jnp.float32, jnp.bfloat16
    dma = pltpu.SemaphoreType.DMA
    smem = pl.BlockSpec(memory_space=pltpu.SMEM)
    total = pl.pallas_call(
        functools.partial(kernel, n, columns),
        out_shape=pltpu.VMEM((rows, depth), f32),
        in_specs=[anywhere, anywhere, vmem, smem, smem],
        out_specs=vmem,
        scratch_shapes=[
            pltpu.VMEM((rows, depth), bf16),
            pltpu.VMEM((rows, depth), bf16),
            pltpu.VMEM((n, LANES, depth), f32),
            pltpu.VMEM((n // 2, rows, 2 * LANES), f32),
            pltpu.VMEM((n, rows + 8, LANES), f32),
            pltpu.VMEM((n, rows + 8, LANES), f32),
            pltpu.VMEM((6 * LANES, depth), bf16),
            pltpu.VMEM((rows, 6 * LANES), bf16),
            pltpu.VMEM((rows, LANES), f32),
            dma((3,)),
            dma((n, 4)),
            dma((n,)),
            dma((n, rows // 256 + 1)),
            dma((n, rows // 256 + 1)),
        ],
        compiler_params=pltpu.CompilerParams(
            collective_id=0, has_side_effects=True, vmem_limit_bytes=55 * 2**20
        ),
        name="pair_exchange",
    )(
        i_factors.reshape(rows, depth), j_factors.reshape(nj * width, depth),
        virt_energy.reshape(1, width), occ_i, occ_j,
    )
    return total.reshape(i_factors.shape)


def transpose_blocks(pair_block, blocks):
    leading = pair_block.shape[:-2]
    height = pair_block.shape[-2]
    width = pair_block.shape[-1]
    parts = pair_block.reshape(leading + (height, blocks, height))
    moved = jnp.swapaxes(parts, -1, -3)
    return moved.reshape(leading + (height, width))


def general(i_factors, j_factors, occ_i, occ_j, virt_energy):
    blocks = lax.axis_size("virt")
    left_rows = i_factors.reshape(-1, i_factors.shape[2])
    density = jnp.zeros(i_factors.shape, jnp.float32)
    whole_energy = lax.all_gather(virt_energy, "virt", axis=0, tiled=True)
    for index in range(j_factors.shape[0]):
        whole_rows = lax.all_gather(j_factors[index], "virt", axis=0, tiled=True)
        pair_block = jnp.dot(left_rows, whole_rows.T, precision=lax.Precision.HIGHEST)
        pair_block = pair_block.reshape(i_factors.shape[0], i_factors.shape[1], whole_rows.shape[0])
        swapped = lax.all_to_all(
            transpose_blocks(pair_block, blocks), "virt", split_axis=2, concat_axis=2, tiled=True
        )
        denominator = (
            virt_energy[None, :, None]
            + whole_energy[None, None, :]
            - occ_i[:, None, None]
            - occ_j[index]
        )
        amplitude = (swapped - 2.0 * pair_block) / denominator
        density = density + jnp.einsum(
            "iab,bp->iap", amplitude, whole_rows, precision=lax.Precision.HIGHEST
        )
    return density


def chip_columns(mesh):
    group = list(mesh.devices.reshape(-1, mesh.shape["virt"])[0])
    if len(group) % 2:
        return 0
    chips = group[::2]
    heights = len({getattr(device, "coords", (0, 0, place))[2] for place, device in enumerate(chips)})
    columns, left = divmod(len(chips), heights)
    return columns if left == 0 and columns in (1, 2) else 0


def body(columns, i_factors, j_factors, occ_i, occ_j, virt_energy):
    ni, width, depth = i_factors.shape
    nj = j_factors.shape[0]
    fits = nj == 2 and nj * width == LANES and (ni * width) % 256 == 0 and depth % 512 == 0
    n = lax.axis_size("virt")
    room = 4 * ni * width * depth * 2 + 4 * n * LANES * (depth + 3 * (ni * width + 8))
    if columns and fits and room < 58 * 2**20:
        return fused(columns, i_factors, j_factors, occ_i, occ_j, virt_energy)
    return general(i_factors, j_factors, occ_i, occ_j, virt_energy)


def solution(mesh):
    placed = (
        P("conf", "virt", None),
        P("conf", "virt", None),
        P("conf"),
        P("conf"),
        P(("conf", "virt")),
    )
    return jax.shard_map(
        functools.partial(body, chip_columns(mesh)),
        mesh=mesh, in_specs=placed, out_specs=P("conf", "virt", None), check_vma=False,
    )
```

```python
import functools

import jax
import jax.numpy as jnp
from jax import lax
from jax.experimental import pallas as pl
from jax.experimental.pallas import tpu as pltpu
from jax.sharding import PartitionSpec as P

LANES = 128
MESH = pl.DeviceIdType.MESH


def split(value):
    high = value.astype(jnp.bfloat16)
    low = (value - high.astype(jnp.float32)).astype(jnp.bfloat16)
    return high, low


def kernel(
    n, columns, i_ref, j_ref, energy_in, occ_i_in, occ_j_in, total, amp_parts, j_parts,
    i_high, i_low, j_all, direct, x_send, x_recv, row_ref, energy_ref, occ_i_ref, occ_j_ref,
    local_sem, j_send_sem, j_recv_sem, x_send_sem, x_recv_sem,
):
    levels = n // 2 // columns
    me = lax.axis_index("virt")
    core = lax.rem(me, 2)
    chip = me // 2
    y = lax.rem(chip, columns)
    z = chip // columns
    rows, depth = i_ref.shape
    pair = 2 * LANES
    tall = 256
    chunks = rows // tall
    halves = 2
    wide = 512

    load_j = pltpu.make_async_copy(j_ref, j_all.at[me], local_sem.at[1])
    load_j.start()
    load_i = pltpu.make_async_copy(i_ref, total, local_sem.at[0])

    barrier = pltpu.get_barrier_semaphore()

    def greet(device):
        pl.semaphore_signal(barrier, inc=1, device_id={"virt": device}, device_id_type=MESH)

    greet(me + 1 - 2 * core)
    if columns == 2:
        greet(me + 2 * (1 - 2 * y))

    @pl.when(z + 1 < levels)
    def _():
        greet(me + 2 * columns)

    @pl.when(z > 0)
    def _():
        greet(me - 2 * columns)

    inner = jnp.logical_and(z > 0, z + 1 < levels)
    load_i.start()
    small = [
        pltpu.make_async_copy(source, target, local_sem.at[3 + place])
        for place, (source, target) in enumerate(
            ((energy_in, energy_ref), (occ_i_in, occ_i_ref), (occ_j_in, occ_j_ref))
        )
    ]
    for copy in small:
        copy.start()
    pl.semaphore_wait(barrier, columns + (inner.astype(jnp.int32) + 1 if levels > 1 else 0))

    def j_copy(origin, half, flow, device):
        part = pl.ds(half * (LANES // halves), LANES // halves)
        return pltpu.make_async_remote_copy(
            src_ref=j_all.at[origin, part],
            dst_ref=j_all.at[origin, part],
            send_sem=j_send_sem.at[flow],
            recv_sem=j_recv_sem.at[origin, half],
            device_id={"virt": device},
            device_id_type=MESH,
        )

    def j_send(origin, half):
        place = origin // 2
        same_core = lax.rem(origin, 2) == core
        in_column = jnp.logical_and(same_core, lax.rem(place, columns) == y)
        from_z = place // columns

        @pl.when(jnp.logical_and(in_column, jnp.logical_and(z >= from_z, z + 1 < levels)))
        def _():
            j_copy(origin, half, 0, me + 2 * columns).start()

        @pl.when(jnp.logical_and(in_column, jnp.logical_and(z <= from_z, z > 0)))
        def _():
            j_copy(origin, half, 0, me - 2 * columns).start()

        if columns == 2:
            @pl.when(in_column)
            def _():
                j_copy(origin, half, 1, me + 2 * (1 - 2 * y)).start()

        @pl.when(same_core)
        def _():
            j_copy(origin, half, 1, me + 1 - 2 * core).start()

    def drain(sent, sem):
        pltpu.make_async_remote_copy(
            src_ref=sent, dst_ref=sent, send_sem=sem, recv_sem=sem,
            device_id={"virt": me}, device_id_type=MESH,
        ).wait_send()

    def inward(at_z):
        return jnp.where(2 * at_z >= levels, -1, 1)

    def last_of(place):
        at_z, at_y = place // columns, lax.rem(place, columns)
        if columns == 2:
            offset = 1 if levels > 1 else 0
        else:
            offset = jnp.maximum(at_z, levels - 1 - at_z)
        return (at_z + inward(at_z) * offset) * columns + columns - 1 - at_y

    def x_rows(chunk):
        return pl.ds(pl.multiple_of(chunk * tall, tall), tall)

    def x_copy(other, origin, part, slot):
        return pltpu.make_async_remote_copy(
            src_ref=x_send.at[other, part],
            dst_ref=x_recv.at[origin, part],
            send_sem=x_send_sem.at[0],
            recv_sem=x_recv_sem.at[slot],
            device_id={"virt": other},
            device_id_type=MESH,
        )

    def x_block(other, chunk):
        late = last_of(other // 2) == chip
        slot = jnp.where(late, n + core * chunks + chunk, me)
        return x_copy(other, me, x_rows(chunk), slot)

    def x_energy(other, origin):
        return x_copy(other, origin, pl.ds(rows, 1), origin)

    def x_stay():
        return pltpu.make_async_copy(x_send.at[me], x_recv.at[me], local_sem.at[2])

    load_j.wait()
    for half in range(halves):
        j_send(me, half)
    load_i.wait()

    @pl.loop(0, rows // 32)
    def _(step):
        part = pl.ds(pl.multiple_of(step * 32, 32), 32)
        high, low = split(total[part, :])
        i_high[part, :] = high
        i_low[part, :] = low
        total[part, :] = jnp.zeros((32, depth), jnp.float32)

    for copy in small:
        copy.wait()
    width = energy_ref.shape[1]
    energy = energy_ref[...]
    twice = jnp.concatenate([energy, energy], axis=1)
    tall_energy = jnp.broadcast_to(twice, (LANES, LANES)).T[:width]
    for orbital in range(rows // width):
        row_ref[orbital * width:(orbital + 1) * width, :] = tall_energy - occ_i_ref[orbital]
    col_lane = lax.broadcasted_iota(jnp.int32, (8, LANES), 1)
    col_term = jnp.broadcast_to(twice, (8, LANES)) - jnp.where(
        col_lane < width, occ_j_ref[0], occ_j_ref[1]
    )

    @pl.loop(0, n)
    def _(other):
        x_send[other, pl.ds(rows, 8), :] = col_term

    def split_j(place, copies):
        per = LANES // 32

        @pl.loop(0, 2 * per)
        def _(step):
            from_rows = pl.ds(pl.multiple_of(lax.rem(step, per) * 32, 32), 32)
            high, low = split(j_all[2 * place + step // per, from_rows, :])
            base = pl.multiple_of(step * 32, 32)
            j_parts[pl.ds(base, 32), :] = high
            j_parts[pl.ds(pair + base, 32), :] = low
            if copies == 3:
                j_parts[pl.ds(2 * pair + base, 32), :] = high

    toward = inward(z)
    deepest = jnp.maximum(z, levels - 1 - z)
    beside = 2 * levels
    visits = beside + (columns - 1) * levels

    def visit(step):
        crossed = step >= beside
        turn = step - beside
        depth_in = jnp.where(turn < deepest - 1, deepest - turn, deepest - 1 - turn)
        if levels > 1:
            depth_in = jnp.where(turn == levels - 1, 1, depth_in)
        distance = step // 2

        def on(way):
            offset = jnp.where(crossed, depth_in, (1 - 2 * way) * distance)
            at_z = z + toward * offset
            valid = jnp.logical_and(at_z >= 0, at_z < levels)
            once = jnp.logical_or(way == 0, jnp.logical_and(step < beside, distance > 0))
            at_y = jnp.where(crossed, columns - 1 - y, y)
            return jnp.logical_and(valid, once), at_z * columns + at_y

        return on, jnp.where(crossed, 0, lax.rem(step, 2))

    @pl.loop(0, visits)
    def _(step):
        on, sign = visit(step)

        @pl.when(sign == 0)
        def _():
            for way in range(2):
                valid, place = on(way)
                origin = 2 * place + core

                @pl.when(jnp.logical_and(valid, origin != me))
                def _():
                    for half in range(halves):
                        j_copy(origin, half, 0, me).wait_recv()
                        j_send(origin, half)

        valid, place = on(sign)

        @pl.when(valid)
        def _():
            for half in range(halves):
                j_copy(2 * place + 1 - core, half, 0, me).wait_recv()
            for side in range(2):
                other = 2 * place + side

                @pl.when(other != me)
                def _():
                    x_energy(other, me).start()

            split_j(place, 2)
            lane = lax.broadcasted_iota(jnp.int32, (LANES // 2, LANES), 1)
            half = LANES // 2
            contract = (((1,), (1,)), ((), ()))

            @pl.loop(0, rows // tall)
            def _(block):
                start = pl.multiple_of(block * tall, tall)
                high, low = i_high[pl.ds(start, tall), :], i_low[pl.ds(start, tall), :]
                j_high, j_low = j_parts[pl.ds(0, pair), :], j_parts[pl.ds(pair, pair), :]
                dot = functools.partial(
                    lax.dot_general, dimension_numbers=contract,
                    preferred_element_type=jnp.float32,
                )
                block_pair = dot(high, j_high) + (dot(high, j_low) + dot(low, j_high))
                direct[place, pl.ds(start, tall), :] = block_pair
                for side in range(2):
                    for group in range(tall // LANES):
                        tile = block_pair[
                            group * LANES:(group + 1) * LANES, side * LANES:(side + 1) * LANES
                        ]
                        turned = tile.T
                        moved = pltpu.roll(turned, half, 1)
                        first = jnp.where(lane < half, turned[:half], moved[half:])
                        second = jnp.where(lane < half, moved[:half], turned[half:])
                        base = start + group * LANES
                        x_send[2 * place + side, pl.ds(base, half), :] = first
                        x_send[2 * place + side, pl.ds(base + half, half), :] = second
                for side in range(2):
                    other = 2 * place + side

                    @pl.when(other != me)
                    def _():
                        x_block(other, block).start()

            for side in range(2):
                other = 2 * place + side

                @pl.when(other == me)
                def _():
                    x_stay().start()

    def await_place(place):
        for side in range(2):
            other = 2 * place + side

            @pl.when(other != me)
            def _():
                x_copy(other, other, pl.ds(0, rows + 1), other).wait_recv()

            @pl.when(other == me)
            def _():
                x_stay().wait()

    def await_late(chunk):
        for side in range(2):
            other = 2 * last_place + side
            x_copy(other, other, x_rows(chunk), n + side * chunks + chunk).wait_recv()

    def amplitudes(place, part):
        for side in range(2):
            other = 2 * place + side
            lanes = slice(side * LANES, (side + 1) * LANES)
            swapped = x_recv[other, part, :]
            own = direct[place, part, lanes]
            denominator = row_ref[part, :] + x_recv[other, pl.ds(rows, 1), :]
            high, low = split((swapped - 2.0 * own) / denominator)
            amp_parts[part, side * LANES:(side + 1) * LANES] = high
            amp_parts[part, pair + side * LANES:pair + (side + 1) * LANES] = high
            amp_parts[part, 2 * pair + side * LANES:2 * pair + (side + 1) * LANES] = low

    last_place = last_of(chip)

    @pl.loop(0, visits)
    def _(step):
        on, sign = visit(step)
        valid, place = on(sign)

        @pl.when(jnp.logical_and(valid, place != last_place))
        def _():
            split_j(place, 3)
            await_place(place)

            @pl.loop(0, chunks)
            def _(block):
                amplitudes(place, x_rows(block))

            @pl.loop(0, depth // pair)
            def _(strip):
                at = pl.ds(pl.multiple_of(strip * pair, pair), pair)
                total[:, at] += jnp.dot(
                    amp_parts[...], j_parts[:, at], preferred_element_type=jnp.float32
                )

    split_j(last_place, 3)

    def j_sent(flow, blocks):
        drain(j_all.at[pl.ds(0, blocks)], j_send_sem.at[flow])

    j_sent(1, n // 2 + (levels if columns == 2 else 0))
    if levels > 1:
        pl.when(inner)(lambda: j_sent(0, levels + 1))
        pl.when(jnp.logical_not(inner))(lambda: j_sent(0, 1))

    for side in range(2):
        x_energy(2 * last_place + side, 2 * last_place + side).wait_recv()

    @pl.loop(0, chunks)
    def _(block):
        part = x_rows(block)
        await_late(block)
        amplitudes(last_place, part)

        @pl.when(block < chunks - 1)
        def _():
            @pl.loop(0, depth // wide)
            def _(strip):
                at = pl.ds(pl.multiple_of(strip * wide, wide), wide)
                total[part, at] += jnp.dot(
                    amp_parts[part, :], j_parts[:, at], preferred_element_type=jnp.float32
                )

    drain(x_send.at[pl.ds(0, n - 1), pl.ds(0, rows + 1)], x_send_sem.at[0])


def finish(total_ref, amp_ref, j_ref, out_ref, last_ref, sems):
    rows, depth = total_ref.shape
    tall = last_ref.shape[0]
    ready = rows // tall - 1
    strips = sems.shape[0] - ready
    wide = depth // strips

    def store(piece):
        part = pl.ds(piece * tall, tall)
        return pltpu.make_async_copy(total_ref.at[part], out_ref.at[part], sems.at[piece])

    def store_last(strip):
        at = pl.ds(strip * wide, wide)
        return pltpu.make_async_copy(
            last_ref.at[:, at], out_ref.at[pl.ds(ready * tall, tall), at], sems.at[ready + strip]
        )

    for piece in range(ready):
        store(piece).start()
    part = slice(ready * tall, rows)
    for strip in range(strips):
        at = slice(strip * wide, (strip + 1) * wide)
        last_ref[:, at] = total_ref[part, at] + jnp.dot(
            amp_ref[part, :], j_ref[:, at], preferred_element_type=jnp.float32
        )
        store_last(strip).start()
    for piece in range(ready):
        store(piece).wait()
    for strip in range(strips):
        store_last(strip).wait()


def fused(columns, i_factors, j_factors, occ_i, occ_j, virt_energy):
    n = lax.axis_size("virt")
    ni, width, depth = i_factors.shape
    nj = j_factors.shape[0]
    rows = ni * width
    anywhere = pl.BlockSpec(memory_space=pl.ANY)
    vmem = pl.BlockSpec(memory_space=pltpu.VMEM)
    f32, bf16 = jnp.float32, jnp.bfloat16
    dma = pltpu.SemaphoreType.DMA
    smem = pltpu.SMEM
    held = pl.pallas_call(
        functools.partial(kernel, n, columns),
        out_shape=(
            pltpu.VMEM((rows, depth), f32),
            pltpu.VMEM((rows, 6 * LANES), bf16),
            pltpu.VMEM((6 * LANES, depth), bf16),
        ),
        in_specs=[anywhere] * 5,
        out_specs=(vmem, vmem, vmem),
        scratch_shapes=[
            pltpu.VMEM((rows, depth), bf16),
            pltpu.VMEM((rows, depth), bf16),
            pltpu.VMEM((n, LANES, depth), f32),
            pltpu.VMEM((n // 2, rows, 2 * LANES), f32),
            pltpu.VMEM((n, rows + 8, LANES), f32),
            pltpu.VMEM((n, rows + 8, LANES), f32),
            pltpu.VMEM((rows, LANES), f32),
            pltpu.VMEM((1, width), f32),
            smem((ni,), f32),
            smem((nj,), f32),
            dma((6,)),
            dma((2,)),
            dma((n, 2)),
            dma((1,)),
            dma((n + 2 * (rows // 256),)),
        ],
        compiler_params=pltpu.CompilerParams(
            collective_id=0, has_side_effects=True, vmem_limit_bytes=50 * 2**20
        ),
        name="pair_exchange",
    )(
        i_factors.reshape(rows, depth), j_factors.reshape(nj * width, depth),
        virt_energy.reshape(1, width), occ_i, occ_j,
    )
    tall = 256
    strips = 8
    out = pl.pallas_call(
        finish,
        out_shape=jax.ShapeDtypeStruct((rows, depth), f32),
        in_specs=[vmem, vmem, vmem],
        out_specs=anywhere,
        scratch_shapes=[pltpu.VMEM((tall, depth), f32), dma((rows // tall - 1 + strips,))],
        compiler_params=pltpu.CompilerParams(vmem_limit_bytes=4 * 2**20),
        name="store",
    )(*[pltpu.with_memory_space_constraint(array, pltpu.VMEM) for array in held])
    return out.reshape(i_factors.shape)


def transpose_blocks(pair_block, blocks):
    leading = pair_block.shape[:-2]
    height = pair_block.shape[-2]
    width = pair_block.shape[-1]
    parts = pair_block.reshape(leading + (height, blocks, height))
    moved = jnp.swapaxes(parts, -1, -3)
    return moved.reshape(leading + (height, width))


def general(i_factors, j_factors, occ_i, occ_j, virt_energy):
    blocks = lax.axis_size("virt")
    left_rows = i_factors.reshape(-1, i_factors.shape[2])
    density = jnp.zeros(i_factors.shape, jnp.float32)
    whole_energy = lax.all_gather(virt_energy, "virt", axis=0, tiled=True)
    for index in range(j_factors.shape[0]):
        whole_rows = lax.all_gather(j_factors[index], "virt", axis=0, tiled=True)
        pair_block = jnp.dot(left_rows, whole_rows.T, precision=lax.Precision.HIGHEST)
        pair_block = pair_block.reshape(i_factors.shape[0], i_factors.shape[1], whole_rows.shape[0])
        swapped = lax.all_to_all(
            transpose_blocks(pair_block, blocks), "virt", split_axis=2, concat_axis=2, tiled=True
        )
        denominator = (
            virt_energy[None, :, None]
            + whole_energy[None, None, :]
            - occ_i[:, None, None]
            - occ_j[index]
        )
        amplitude = (swapped - 2.0 * pair_block) / denominator
        density = density + jnp.einsum(
            "iab,bp->iap", amplitude, whole_rows, precision=lax.Precision.HIGHEST
        )
    return density


def chip_columns(mesh):
    group = list(mesh.devices.reshape(-1, mesh.shape["virt"])[0])
    if len(group) % 2:
        return 0
    chips = group[::2]
    heights = len({getattr(device, "coords", (0, 0, place))[2] for place, device in enumerate(chips)})
    columns, left = divmod(len(chips), heights)
    return columns if left == 0 and columns in (1, 2) else 0


def body(columns, i_factors, j_factors, occ_i, occ_j, virt_energy):
    ni, width, depth = i_factors.shape
    nj = j_factors.shape[0]
    fits = nj == 2 and nj * width == LANES and (ni * width) % 256 == 0 and depth % 512 == 0
    n = lax.axis_size("virt")
    room = 4 * ni * width * depth * 2 + 4 * n * LANES * (depth + 3 * (ni * width + 8))
    if columns and fits and room < 58 * 2**20:
        return fused(columns, i_factors, j_factors, occ_i, occ_j, virt_energy)
    return general(i_factors, j_factors, occ_i, occ_j, virt_energy)


def solution(mesh):
    placed = (
        P("conf", "virt", None),
        P("conf", "virt", None),
        P("conf"),
        P("conf"),
        P(("conf", "virt")),
    )
    return jax.shard_map(
        functools.partial(body, chip_columns(mesh)),
        mesh=mesh, in_specs=placed, out_specs=P("conf", "virt", None), check_vma=False,
    )
```

```python
import functools

import jax
import jax.numpy as jnp
from jax import lax
from jax.experimental import pallas as pl
from jax.experimental.pallas import tpu as pltpu
from jax.sharding import PartitionSpec as P

LANES = 128
MESH = pl.DeviceIdType.MESH


def split(value):
    high = value.astype(jnp.bfloat16)
    low = (value - high.astype(jnp.float32)).astype(jnp.bfloat16)
    return high, low


def kernel(
    n, i_ref, j_ref, energy_in, occ_i_in, occ_j_in, total, amp_parts, j_parts,
    i_high, i_low, j_all, direct, x_send, x_recv, row_ref, energy_ref, occ_i_ref, occ_j_ref,
    local_sem, j_send_sem, j_recv_sem, x_send_sem, x_recv_sem,
):
    columns = 2
    levels = n // 2 // columns
    me = lax.axis_index("virt")
    core = lax.rem(me, 2)
    chip = me // 2
    y = lax.rem(chip, columns)
    z = chip // columns
    rows, depth = i_ref.shape
    pair = 2 * LANES
    tall = 256
    chunks = rows // tall
    halves = 2
    wide = 512

    load_j = pltpu.make_async_copy(j_ref, j_all.at[me], local_sem.at[1])
    load_j.start()
    load_i = pltpu.make_async_copy(i_ref, total, local_sem.at[0])

    barrier = pltpu.get_barrier_semaphore()

    def greet(device):
        pl.semaphore_signal(barrier, inc=1, device_id={"virt": device}, device_id_type=MESH)

    greet(me + 1 - 2 * core)
    greet(me + 2 * (1 - 2 * y))

    @pl.when(z + 1 < levels)
    def _():
        greet(me + 2 * columns)

    @pl.when(z > 0)
    def _():
        greet(me - 2 * columns)

    inner = jnp.logical_and(z > 0, z + 1 < levels)
    load_i.start()
    small = [
        pltpu.make_async_copy(source, target, local_sem.at[3 + place])
        for place, (source, target) in enumerate(
            ((energy_in, energy_ref), (occ_i_in, occ_i_ref), (occ_j_in, occ_j_ref))
        )
    ]
    for copy in small:
        copy.start()
    pl.semaphore_wait(barrier, 3 + inner.astype(jnp.int32))

    def j_copy(origin, half, flow, device):
        part = pl.ds(half * (LANES // halves), LANES // halves)
        ahead = flow == 0 and half == 0
        slot = n + origin // 2 // columns if ahead else origin
        return pltpu.make_async_remote_copy(
            src_ref=j_all.at[origin, part],
            dst_ref=j_all.at[origin, part],
            send_sem=j_send_sem.at[flow],
            recv_sem=j_recv_sem.at[slot],
            device_id={"virt": device},
            device_id_type=MESH,
        )

    def j_await(origin):
        whole = j_all.at[origin]
        pltpu.make_async_remote_copy(
            src_ref=whole, dst_ref=whole, send_sem=j_send_sem.at[1], recv_sem=j_recv_sem.at[origin],
            device_id={"virt": me}, device_id_type=MESH,
        ).wait_recv()

    def j_send(origin, half):
        place = origin // 2
        same_core = lax.rem(origin, 2) == core
        in_column = jnp.logical_and(same_core, lax.rem(place, columns) == y)
        from_z = place // columns

        @pl.when(jnp.logical_and(in_column, jnp.logical_and(z >= from_z, z + 1 < levels)))
        def _():
            j_copy(origin, half, 0, me + 2 * columns).start()

        @pl.when(jnp.logical_and(in_column, jnp.logical_and(z <= from_z, z > 0)))
        def _():
            j_copy(origin, half, 0, me - 2 * columns).start()

        @pl.when(in_column)
        def _():
            j_copy(origin, half, 1, me + 2 * (1 - 2 * y)).start()

        @pl.when(same_core)
        def _():
            j_copy(origin, half, 1, me + 1 - 2 * core).start()

    def drain(sent, sem):
        pltpu.make_async_remote_copy(
            src_ref=sent, dst_ref=sent, send_sem=sem, recv_sem=sem,
            device_id={"virt": me}, device_id_type=MESH,
        ).wait_send()

    def inward(at_z):
        return jnp.where(2 * at_z >= levels, -1, 1)

    def ahead_of(place):
        return place + inward(place // columns) * columns

    def across(place):
        return place + 1 - 2 * lax.rem(place, columns)

    def x_rows(chunk):
        return pl.ds(pl.multiple_of(chunk * tall, tall), tall)

    def x_copy(other, origin, part, slot):
        return pltpu.make_async_remote_copy(
            src_ref=x_send.at[other, part],
            dst_ref=x_recv.at[origin, part],
            send_sem=x_send_sem.at[0],
            recv_sem=x_recv_sem.at[slot],
            device_id={"virt": other},
            device_id_type=MESH,
        )

    def x_block(other, chunk):
        late = across(ahead_of(other // 2)) == chip
        slot = jnp.where(late, n // 2 + core * chunks + chunk, chip)
        return x_copy(other, me, x_rows(chunk), slot)

    def x_held(other, origin):
        return x_copy(
            other, origin, x_rows(chunks - 1), n // 2 + 2 * chunks + lax.rem(origin, 2)
        )

    def x_energy(other):
        return x_copy(other, me, pl.ds(rows, 1), chip)

    def x_await(place, first, sides, count):
        block = x_recv.at[pl.ds(first, sides), pl.ds(0, count)]
        pltpu.make_async_remote_copy(
            src_ref=block, dst_ref=block, send_sem=x_send_sem.at[0], recv_sem=x_recv_sem.at[place],
            device_id={"virt": me}, device_id_type=MESH,
        ).wait_recv()

    def x_stay():
        return pltpu.make_async_copy(x_send.at[me], x_recv.at[me], local_sem.at[2])

    load_j.wait()
    for half in range(halves):
        j_send(me, half)
    load_i.wait()

    @pl.loop(0, rows // 32)
    def _(step):
        part = pl.ds(pl.multiple_of(step * 32, 32), 32)
        high, low = split(total[part, :])
        i_high[part, :] = high
        i_low[part, :] = low
        total[part, :] = jnp.zeros((32, depth), jnp.float32)

    for copy in small:
        copy.wait()
    width = energy_ref.shape[1]
    energy = energy_ref[...]
    twice = jnp.concatenate([energy, energy], axis=1)
    tall_energy = jnp.broadcast_to(twice, (LANES, LANES)).T[:width]
    for orbital in range(rows // width):
        row_ref[orbital * width:(orbital + 1) * width, :] = tall_energy - occ_i_ref[orbital]
    col_lane = lax.broadcasted_iota(jnp.int32, (8, LANES), 1)
    col_term = jnp.broadcast_to(twice, (8, LANES)) - jnp.where(
        col_lane < width, occ_j_ref[0], occ_j_ref[1]
    )

    @pl.loop(0, n)
    def _(other):
        x_send[other, pl.ds(rows, 8), :] = col_term

    def split_j(place, copies):
        per = LANES // 32

        @pl.loop(0, 2 * per)
        def _(step):
            from_rows = pl.ds(pl.multiple_of(lax.rem(step, per) * 32, 32), 32)
            high, low = split(j_all[2 * place + step // per, from_rows, :])
            base = pl.multiple_of(step * 32, 32)
            j_parts[pl.ds(base, 32), :] = high
            j_parts[pl.ds(pair + base, 32), :] = low
            if copies == 3:
                j_parts[pl.ds(2 * pair + base, 32), :] = high

    toward = inward(z)
    deepest = jnp.maximum(z, levels - 1 - z)
    beside = 2 * levels
    visits = beside + levels

    def visit(step):
        crossed = step >= beside
        turn = step - beside
        depth_in = jnp.where(turn < deepest - 1, deepest - turn, deepest - 1 - turn)
        depth_in = jnp.where(turn == levels - 1, 1, depth_in)
        distance = step // 2

        def on(way):
            offset = jnp.where(crossed, depth_in, (1 - 2 * way) * distance)
            at_z = z + toward * offset
            valid = jnp.logical_and(at_z >= 0, at_z < levels)
            once = jnp.logical_or(way == 0, jnp.logical_and(step < beside, distance > 0))
            at_y = jnp.where(crossed, columns - 1 - y, y)
            return jnp.logical_and(valid, once), at_z * columns + at_y

        return on, jnp.where(crossed, 0, lax.rem(step, 2))

    @pl.loop(0, visits)
    def _(step):
        on, sign = visit(step)

        @pl.when(sign == 0)
        def _():
            for way in range(2):
                valid, place = on(way)
                origin = 2 * place + core

                @pl.when(jnp.logical_and(jnp.logical_and(valid, step < beside), origin != me))
                def _():
                    for half in range(halves):
                        j_copy(origin, half, 0, me).wait_recv()
                        j_send(origin, half)

            _, place = on(0)
            origin = 2 * place + core

            @pl.when(step >= beside)
            def _():
                j_await(origin)
                for half in range(halves):
                    j_send(origin, half)

        valid, place = on(sign)

        @pl.when(valid)
        def _():
            j_await(2 * place + 1 - core)
            for side in range(2):
                other = 2 * place + side

                @pl.when(other != me)
                def _():
                    x_energy(other).start()

            split_j(place, 2)
            lane = lax.broadcasted_iota(jnp.int32, (LANES // 2, LANES), 1)
            half = LANES // 2
            contract = (((1,), (1,)), ((), ()))

            @pl.loop(0, rows // tall)
            def _(block):
                start = pl.multiple_of(block * tall, tall)
                high, low = i_high[pl.ds(start, tall), :], i_low[pl.ds(start, tall), :]
                j_high, j_low = j_parts[pl.ds(0, pair), :], j_parts[pl.ds(pair, pair), :]
                dot = functools.partial(
                    lax.dot_general, dimension_numbers=contract,
                    preferred_element_type=jnp.float32,
                )
                block_pair = dot(high, j_high) + (dot(high, j_low) + dot(low, j_high))
                direct[place, pl.ds(start, tall), :] = block_pair
                for side in range(2):
                    for group in range(tall // LANES):
                        tile = block_pair[
                            group * LANES:(group + 1) * LANES, side * LANES:(side + 1) * LANES
                        ]
                        turned = tile.T
                        moved = pltpu.roll(turned, half, 1)
                        first = jnp.where(lane < half, turned[:half], moved[half:])
                        second = jnp.where(lane < half, moved[:half], turned[half:])
                        base = start + group * LANES
                        x_send[2 * place + side, pl.ds(base, half), :] = first
                        x_send[2 * place + side, pl.ds(base + half, half), :] = second
                hold = jnp.logical_and(ahead_of(place) == chip, block == chunks - 1)
                for side in range(2):
                    other = 2 * place + side

                    @pl.when(jnp.logical_and(other != me, jnp.logical_not(hold)))
                    def _():
                        x_block(other, block).start()

            for side in range(2):
                other = 2 * place + side

                @pl.when(other == me)
                def _():
                    x_stay().start()

    for way in (-1, 1):
        place = chip + way * columns
        there = jnp.logical_and(z + way >= 0, z + way < levels)

        @pl.when(jnp.logical_and(there, ahead_of(place) == chip))
        def _():
            for side in range(2):
                x_held(2 * place + side, me).start()

    last_place = ahead_of(chip)
    late_place = across(last_place)

    def await_place(place):
        @pl.when(place == chip)
        def _():
            x_await(chip, me + 1 - 2 * core, 1, rows + 1)
            x_stay().wait()

        @pl.when(place == last_place)
        def _():
            x_await(place, 2 * place, 2, rows - tall + 1)

        @pl.when(jnp.logical_and(place != chip, place != last_place))
        def _():
            x_await(place, 2 * place, 2, rows + 1)

    def await_late(chunk):
        for side in range(2):
            other = 2 * late_place + side
            x_copy(other, other, x_rows(chunk), n // 2 + side * chunks + chunk).wait_recv()

    def amplitudes(place, part):
        for side in range(2):
            other = 2 * place + side
            lanes = slice(side * LANES, (side + 1) * LANES)
            swapped = x_recv[other, part, :]
            own = direct[place, part, lanes]
            denominator = row_ref[part, :] + x_recv[other, pl.ds(rows, 1), :]
            high, low = split((swapped - 2.0 * own) / denominator)
            amp_parts[part, side * LANES:(side + 1) * LANES] = high
            amp_parts[part, pair + side * LANES:pair + (side + 1) * LANES] = high
            amp_parts[part, 2 * pair + side * LANES:2 * pair + (side + 1) * LANES] = low

    @pl.loop(0, visits)
    def _(step):
        on, sign = visit(step)
        valid, place = on(sign)

        @pl.when(jnp.logical_and(valid, place != late_place))
        def _():
            split_j(place, 3)
            await_place(place)
            arrived = jnp.where(place == last_place, chunks - 1, chunks)

            @pl.loop(0, arrived)
            def _(block):
                amplitudes(place, x_rows(block))

            @pl.when(place == last_place)
            def _():
                amp_parts[rows - tall:, :] = jnp.zeros((tall, 3 * pair), jnp.bfloat16)

            @pl.loop(0, depth // pair)
            def _(strip):
                at = pl.ds(pl.multiple_of(strip * pair, pair), pair)
                total[:, at] += jnp.dot(
                    amp_parts[...], j_parts[:, at], preferred_element_type=jnp.float32
                )

    split_j(late_place, 3)

    def j_sent(flow, blocks):
        drain(j_all.at[pl.ds(0, blocks)], j_send_sem.at[flow])

    j_sent(1, n // 2 + levels)
    pl.when(inner)(lambda: j_sent(0, levels + 1))
    pl.when(jnp.logical_not(inner))(lambda: j_sent(0, 1))
    x_await(late_place, 2 * late_place, 2, 1)

    @pl.loop(0, chunks)
    def _(block):
        part = x_rows(block)
        await_late(block)
        amplitudes(late_place, part)

        @pl.loop(0, depth // wide)
        def _(strip):
            at = pl.ds(pl.multiple_of(strip * wide, wide), wide)
            total[part, at] += jnp.dot(
                amp_parts[part, :], j_parts[:, at], preferred_element_type=jnp.float32
            )

    split_j(last_place, 3)
    for side in range(2):
        x_held(2 * last_place + side, 2 * last_place + side).wait_recv()
    amplitudes(last_place, slice(rows - tall, rows))
    drain(x_send.at[pl.ds(0, n - 1), pl.ds(0, rows + 1)], x_send_sem.at[0])


def finish(total_ref, amp_ref, j_ref, out_ref, last_ref, sems):
    rows, depth = total_ref.shape
    tall = last_ref.shape[0]
    ready = rows // tall - 1
    strips = sems.shape[0] - ready
    wide = depth // strips

    def store(piece):
        part = pl.ds(piece * tall, tall)
        return pltpu.make_async_copy(total_ref.at[part], out_ref.at[part], sems.at[piece])

    def store_last(strip):
        at = pl.ds(strip * wide, wide)
        return pltpu.make_async_copy(
            last_ref.at[:, at], out_ref.at[pl.ds(ready * tall, tall), at], sems.at[ready + strip]
        )

    for piece in range(ready):
        store(piece).start()
    part = slice(ready * tall, rows)
    for strip in range(strips):
        at = slice(strip * wide, (strip + 1) * wide)
        last_ref[:, at] = total_ref[part, at] + jnp.dot(
            amp_ref[part, :], j_ref[:, at], preferred_element_type=jnp.float32
        )
        store_last(strip).start()
    for piece in range(ready):
        store(piece).wait()
    for strip in range(strips):
        store_last(strip).wait()


def fused(i_factors, j_factors, occ_i, occ_j, virt_energy):
    n = lax.axis_size("virt")
    ni, width, depth = i_factors.shape
    nj = j_factors.shape[0]
    rows = ni * width
    anywhere = pl.BlockSpec(memory_space=pl.ANY)
    vmem = pl.BlockSpec(memory_space=pltpu.VMEM)
    f32, bf16 = jnp.float32, jnp.bfloat16
    dma = pltpu.SemaphoreType.DMA
    smem = pltpu.SMEM
    held = pl.pallas_call(
        functools.partial(kernel, n),
        out_shape=(
            pltpu.VMEM((rows, depth), f32),
            pltpu.VMEM((rows, 6 * LANES), bf16),
            pltpu.VMEM((6 * LANES, depth), bf16),
        ),
        in_specs=[anywhere] * 5,
        out_specs=(vmem, vmem, vmem),
        scratch_shapes=[
            pltpu.VMEM((rows, depth), bf16),
            pltpu.VMEM((rows, depth), bf16),
            pltpu.VMEM((n, LANES, depth), f32),
            pltpu.VMEM((n // 2, rows, 2 * LANES), f32),
            pltpu.VMEM((n, rows + 8, LANES), f32),
            pltpu.VMEM((n, rows + 8, LANES), f32),
            pltpu.VMEM((rows, LANES), f32),
            pltpu.VMEM((1, width), f32),
            smem((ni,), f32),
            smem((nj,), f32),
            dma((6,)),
            dma((2,)),
            dma((n + n // 4,)),
            dma((1,)),
            dma((n // 2 + 2 * (rows // 256) + 2,)),
        ],
        compiler_params=pltpu.CompilerParams(
            collective_id=0, has_side_effects=True, vmem_limit_bytes=50 * 2**20
        ),
        name="pair_exchange",
    )(
        i_factors.reshape(rows, depth), j_factors.reshape(nj * width, depth),
        virt_energy.reshape(1, width), occ_i, occ_j,
    )
    tall = 256
    strips = 8
    out = pl.pallas_call(
        finish,
        out_shape=jax.ShapeDtypeStruct((rows, depth), f32),
        in_specs=[vmem, vmem, vmem],
        out_specs=anywhere,
        scratch_shapes=[pltpu.VMEM((tall, depth), f32), dma((rows // tall - 1 + strips,))],
        compiler_params=pltpu.CompilerParams(vmem_limit_bytes=4 * 2**20),
        name="store",
    )(*[pltpu.with_memory_space_constraint(array, pltpu.VMEM) for array in held])
    return out.reshape(i_factors.shape)


def transpose_blocks(pair_block, blocks):
    leading = pair_block.shape[:-2]
    height = pair_block.shape[-2]
    width = pair_block.shape[-1]
    parts = pair_block.reshape(leading + (height, blocks, height))
    moved = jnp.swapaxes(parts, -1, -3)
    return moved.reshape(leading + (height, width))


def general(i_factors, j_factors, occ_i, occ_j, virt_energy):
    blocks = lax.axis_size("virt")
    left_rows = i_factors.reshape(-1, i_factors.shape[2])
    density = jnp.zeros(i_factors.shape, jnp.float32)
    whole_energy = lax.all_gather(virt_energy, "virt", axis=0, tiled=True)
    for index in range(j_factors.shape[0]):
        whole_rows = lax.all_gather(j_factors[index], "virt", axis=0, tiled=True)
        pair_block = jnp.dot(left_rows, whole_rows.T, precision=lax.Precision.HIGHEST)
        pair_block = pair_block.reshape(i_factors.shape[0], i_factors.shape[1], whole_rows.shape[0])
        swapped = lax.all_to_all(
            transpose_blocks(pair_block, blocks), "virt", split_axis=2, concat_axis=2, tiled=True
        )
        denominator = (
            virt_energy[None, :, None]
            + whole_energy[None, None, :]
            - occ_i[:, None, None]
            - occ_j[index]
        )
        amplitude = (swapped - 2.0 * pair_block) / denominator
        density = density + jnp.einsum(
            "iab,bp->iap", amplitude, whole_rows, precision=lax.Precision.HIGHEST
        )
    return density


def chip_columns(mesh):
    group = list(mesh.devices.reshape(-1, mesh.shape["virt"])[0])
    if len(group) % 2:
        return 0
    chips = group[::2]
    heights = len({getattr(device, "coords", (0, 0, place))[2] for place, device in enumerate(chips)})
    columns, left = divmod(len(chips), heights)
    return columns if left == 0 and columns in (1, 2) else 0


def body(columns, i_factors, j_factors, occ_i, occ_j, virt_energy):
    ni, width, depth = i_factors.shape
    nj = j_factors.shape[0]
    fits = nj == 2 and nj * width == LANES and (ni * width) % 256 == 0 and depth % 512 == 0
    n = lax.axis_size("virt")
    tall_enough = columns == 2 and n // 4 >= 2
    room = 4 * ni * width * depth * 2 + 4 * n * LANES * (depth + 3 * (ni * width + 8))
    if tall_enough and fits and room < 58 * 2**20:
        return fused(i_factors, j_factors, occ_i, occ_j, virt_energy)
    return general(i_factors, j_factors, occ_i, occ_j, virt_energy)


def solution(mesh):
    placed = (
        P("conf", "virt", None),
        P("conf", "virt", None),
        P("conf"),
        P("conf"),
        P(("conf", "virt")),
    )
    return jax.shard_map(
        functools.partial(body, chip_columns(mesh)),
        mesh=mesh, in_specs=placed, out_specs=P("conf", "virt", None), check_vma=False,
    )
```

```python
import functools

import jax
import jax.numpy as jnp
from jax import lax
from jax.experimental import pallas as pl
from jax.experimental.pallas import tpu as pltpu
from jax.sharding import PartitionSpec as P

LANES = 128
MESH = pl.DeviceIdType.MESH


def split(value):
    high = value.astype(jnp.bfloat16)
    low = (value - high.astype(jnp.float32)).astype(jnp.bfloat16)
    return high, low


def kernel(
    n, i_ref, j_ref, energy_in, occ_i_in, occ_j_in, total, amp_parts, j_parts,
    i_high, i_low, j_all, direct, x_send, x_recv, row_ref, energy_ref, occ_i_ref, occ_j_ref,
    local_sem, j_send_sem, j_recv_sem, x_send_sem, x_recv_sem,
):
    columns = 2
    levels = n // 2 // columns
    me = lax.axis_index("virt")
    core = lax.rem(me, 2)
    chip = me // 2
    y = lax.rem(chip, columns)
    z = chip // columns
    rows, depth = i_ref.shape
    pair = 2 * LANES
    tall = 256
    chunks = rows // tall
    halves = 2
    wide = 512

    load_j = pltpu.make_async_copy(j_ref, j_all.at[me], local_sem.at[1])
    load_j.start()
    load_i = pltpu.make_async_copy(i_ref, total, local_sem.at[0])

    barrier = pltpu.get_barrier_semaphore()

    def greet(device):
        pl.semaphore_signal(barrier, inc=1, device_id={"virt": device}, device_id_type=MESH)

    greet(me + 1 - 2 * core)
    greet(me + 2 * (1 - 2 * y))

    @pl.when(z + 1 < levels)
    def _():
        greet(me + 2 * columns)

    @pl.when(z > 0)
    def _():
        greet(me - 2 * columns)

    inner = jnp.logical_and(z > 0, z + 1 < levels)
    load_i.start()
    small = [
        pltpu.make_async_copy(source, target, local_sem.at[3 + place])
        for place, (source, target) in enumerate(
            ((energy_in, energy_ref), (occ_i_in, occ_i_ref), (occ_j_in, occ_j_ref))
        )
    ]
    for copy in small:
        copy.start()
    pl.semaphore_wait(barrier, 3 + inner.astype(jnp.int32))

    def j_copy(origin, half, flow, device):
        part = pl.ds(half * (LANES // halves), LANES // halves)
        ahead = flow == 0 and half == 0
        slot = n + origin // 2 // columns if ahead else origin
        return pltpu.make_async_remote_copy(
            src_ref=j_all.at[origin, part],
            dst_ref=j_all.at[origin, part],
            send_sem=j_send_sem.at[flow],
            recv_sem=j_recv_sem.at[slot],
            device_id={"virt": device},
            device_id_type=MESH,
        )

    def j_await(origin):
        whole = j_all.at[origin]
        pltpu.make_async_remote_copy(
            src_ref=whole, dst_ref=whole, send_sem=j_send_sem.at[1], recv_sem=j_recv_sem.at[origin],
            device_id={"virt": me}, device_id_type=MESH,
        ).wait_recv()

    def j_send(origin, half):
        place = origin // 2
        same_core = lax.rem(origin, 2) == core
        in_column = jnp.logical_and(same_core, lax.rem(place, columns) == y)
        from_z = place // columns

        @pl.when(jnp.logical_and(in_column, jnp.logical_and(z >= from_z, z + 1 < levels)))
        def _():
            j_copy(origin, half, 0, me + 2 * columns).start()

        @pl.when(jnp.logical_and(in_column, jnp.logical_and(z <= from_z, z > 0)))
        def _():
            j_copy(origin, half, 0, me - 2 * columns).start()

        @pl.when(in_column)
        def _():
            j_copy(origin, half, 1, me + 2 * (1 - 2 * y)).start()

        @pl.when(same_core)
        def _():
            j_copy(origin, half, 1, me + 1 - 2 * core).start()

    def drain(sent, sem):
        pltpu.make_async_remote_copy(
            src_ref=sent, dst_ref=sent, send_sem=sem, recv_sem=sem,
            device_id={"virt": me}, device_id_type=MESH,
        ).wait_send()

    def inward(at_z):
        return jnp.where(2 * at_z >= levels, -1, 1)

    def ahead_of(place):
        return place + inward(place // columns) * columns

    def across(place):
        return place + 1 - 2 * lax.rem(place, columns)

    def x_rows(chunk):
        return pl.ds(pl.multiple_of(chunk * tall, tall), tall)

    def x_copy(other, origin, part, slot):
        return pltpu.make_async_remote_copy(
            src_ref=x_send.at[other, part],
            dst_ref=x_recv.at[origin, part],
            send_sem=x_send_sem.at[0],
            recv_sem=x_recv_sem.at[slot],
            device_id={"virt": other},
            device_id_type=MESH,
        )

    def x_block(other, chunk):
        late = across(ahead_of(other // 2)) == chip
        slot = jnp.where(late, n // 2 + chunk, chip)
        return x_copy(other, me, x_rows(chunk), slot)

    def x_held(other):
        return x_copy(other, me, x_rows(chunks - 1), n // 2 + chunks)

    def x_energy(other):
        return x_copy(other, me, pl.ds(rows, 1), chip)

    def x_await(slot, first, sides, count):
        block = x_recv.at[pl.ds(first, sides), pl.ds(0, count)]
        pltpu.make_async_remote_copy(
            src_ref=block, dst_ref=block, send_sem=x_send_sem.at[0], recv_sem=x_recv_sem.at[slot],
            device_id={"virt": me}, device_id_type=MESH,
        ).wait_recv()

    def x_stay():
        return pltpu.make_async_copy(x_send.at[me], x_recv.at[me], local_sem.at[2])

    load_j.wait()
    for half in range(halves):
        j_send(me, half)
    load_i.wait()

    @pl.loop(0, rows // 32)
    def _(step):
        part = pl.ds(pl.multiple_of(step * 32, 32), 32)
        high, low = split(total[part, :])
        i_high[part, :] = high
        i_low[part, :] = low
        total[part, :] = jnp.zeros((32, depth), jnp.float32)

    for copy in small:
        copy.wait()
    width = energy_ref.shape[1]
    energy = energy_ref[...]
    twice = jnp.concatenate([energy, energy], axis=1)
    tall_energy = jnp.broadcast_to(twice, (LANES, LANES)).T[:width]
    for orbital in range(rows // width):
        row_ref[orbital * width:(orbital + 1) * width, :] = tall_energy - occ_i_ref[orbital]
    col_lane = lax.broadcasted_iota(jnp.int32, (8, LANES), 1)
    col_term = jnp.broadcast_to(twice, (8, LANES)) - jnp.where(
        col_lane < width, occ_j_ref[0], occ_j_ref[1]
    )

    @pl.loop(0, n)
    def _(other):
        x_send[other, pl.ds(rows, 8), :] = col_term

    def split_j(place, copies):
        per = LANES // 32

        @pl.loop(0, 2 * per)
        def _(step):
            from_rows = pl.ds(pl.multiple_of(lax.rem(step, per) * 32, 32), 32)
            high, low = split(j_all[2 * place + step // per, from_rows, :])
            base = pl.multiple_of(step * 32, 32)
            j_parts[pl.ds(base, 32), :] = high
            j_parts[pl.ds(pair + base, 32), :] = low
            if copies == 3:
                j_parts[pl.ds(2 * pair + base, 32), :] = high

    toward = inward(z)
    deepest = jnp.maximum(z, levels - 1 - z)
    beside = 2 * levels
    visits = beside + levels

    def visit(step):
        crossed = step >= beside
        turn = step - beside
        depth_in = jnp.where(turn < deepest - 1, deepest - turn, deepest - 1 - turn)
        depth_in = jnp.where(turn == levels - 1, 1, depth_in)
        distance = step // 2

        def on(way):
            offset = jnp.where(crossed, depth_in, (1 - 2 * way) * distance)
            at_z = z + toward * offset
            valid = jnp.logical_and(at_z >= 0, at_z < levels)
            once = jnp.logical_or(way == 0, jnp.logical_and(step < beside, distance > 0))
            at_y = jnp.where(crossed, columns - 1 - y, y)
            return jnp.logical_and(valid, once), at_z * columns + at_y

        return on, jnp.where(crossed, 0, lax.rem(step, 2))

    @pl.loop(0, visits)
    def _(step):
        on, sign = visit(step)

        @pl.when(sign == 0)
        def _():
            for way in range(2):
                valid, place = on(way)
                origin = 2 * place + core

                @pl.when(jnp.logical_and(jnp.logical_and(valid, step < beside), origin != me))
                def _():
                    for half in range(halves):
                        j_copy(origin, half, 0, me).wait_recv()
                        j_send(origin, half)

            _, place = on(0)
            origin = 2 * place + core

            @pl.when(step >= beside)
            def _():
                j_await(origin)
                for half in range(halves):
                    j_send(origin, half)

        valid, place = on(sign)

        @pl.when(valid)
        def _():
            j_await(2 * place + 1 - core)
            pieces = jnp.logical_or(ahead_of(place) == chip, across(ahead_of(place)) == chip)
            for side in range(2):
                other = 2 * place + side

                @pl.when(jnp.logical_and(other != me, pieces))
                def _():
                    x_energy(other).start()

            split_j(place, 2)
            lane = lax.broadcasted_iota(jnp.int32, (LANES // 2, LANES), 1)
            half = LANES // 2
            contract = (((1,), (1,)), ((), ()))

            @pl.loop(0, rows // tall)
            def _(block):
                start = pl.multiple_of(block * tall, tall)
                high, low = i_high[pl.ds(start, tall), :], i_low[pl.ds(start, tall), :]
                j_high, j_low = j_parts[pl.ds(0, pair), :], j_parts[pl.ds(pair, pair), :]
                dot = functools.partial(
                    lax.dot_general, dimension_numbers=contract,
                    preferred_element_type=jnp.float32,
                )
                block_pair = dot(high, j_high) + (dot(high, j_low) + dot(low, j_high))
                direct[place, pl.ds(start, tall), :] = block_pair
                for side in range(2):
                    for group in range(tall // LANES):
                        tile = block_pair[
                            group * LANES:(group + 1) * LANES, side * LANES:(side + 1) * LANES
                        ]
                        turned = tile.T
                        moved = pltpu.roll(turned, half, 1)
                        first = jnp.where(lane < half, turned[:half], moved[half:])
                        second = jnp.where(lane < half, moved[:half], turned[half:])
                        base = start + group * LANES
                        x_send[2 * place + side, pl.ds(base, half), :] = first
                        x_send[2 * place + side, pl.ds(base + half, half), :] = second
                hold = jnp.logical_and(ahead_of(place) == chip, block == chunks - 1)
                for side in range(2):
                    other = 2 * place + side

                    by_piece = jnp.logical_and(pieces, jnp.logical_not(hold))

                    @pl.when(jnp.logical_and(other != me, by_piece))
                    def _():
                        x_block(other, block).start()

                    done = jnp.logical_and(jnp.logical_not(pieces), block == chunks - 1)

                    @pl.when(jnp.logical_and(other != me, done))
                    def _():
                        x_copy(other, me, pl.ds(0, rows + 1), chip).start()

            for side in range(2):
                other = 2 * place + side

                @pl.when(other == me)
                def _():
                    x_stay().start()

    for way in (-1, 1):
        place = chip + way * columns
        there = jnp.logical_and(z + way >= 0, z + way < levels)

        @pl.when(jnp.logical_and(there, ahead_of(place) == chip))
        def _():
            for side in range(2):
                x_held(2 * place + side).start()

    last_place = ahead_of(chip)
    late_place = across(last_place)

    def await_place(place):
        @pl.when(place == chip)
        def _():
            x_await(chip, me + 1 - 2 * core, 1, rows + 1)
            x_stay().wait()

        @pl.when(place == last_place)
        def _():
            x_await(place, 2 * place, 2, rows - tall + 1)

        @pl.when(jnp.logical_and(place != chip, place != last_place))
        def _():
            x_await(place, 2 * place, 2, rows + 1)

    def amplitudes(place, part):
        for side in range(2):
            other = 2 * place + side
            lanes = slice(side * LANES, (side + 1) * LANES)
            swapped = x_recv[other, part, :]
            own = direct[place, part, lanes]
            denominator = row_ref[part, :] + x_recv[other, pl.ds(rows, 1), :]
            high, low = split((swapped - 2.0 * own) / denominator)
            amp_parts[part, side * LANES:(side + 1) * LANES] = high
            amp_parts[part, pair + side * LANES:pair + (side + 1) * LANES] = high
            amp_parts[part, 2 * pair + side * LANES:2 * pair + (side + 1) * LANES] = low

    @pl.loop(0, visits)
    def _(step):
        on, sign = visit(step)
        valid, place = on(sign)

        @pl.when(jnp.logical_and(valid, place != late_place))
        def _():
            split_j(place, 3)
            await_place(place)
            arrived = jnp.where(place == last_place, chunks - 1, chunks)

            @pl.loop(0, arrived)
            def _(block):
                amplitudes(place, x_rows(block))

            @pl.when(place == last_place)
            def _():
                amp_parts[rows - tall:, :] = jnp.zeros((tall, 3 * pair), jnp.bfloat16)

            @pl.loop(0, depth // pair)
            def _(strip):
                at = pl.ds(pl.multiple_of(strip * pair, pair), pair)
                total[:, at] += jnp.dot(
                    amp_parts[...], j_parts[:, at], preferred_element_type=jnp.float32
                )

    split_j(late_place, 3)

    def j_sent(flow, blocks):
        drain(j_all.at[pl.ds(0, blocks)], j_send_sem.at[flow])

    j_sent(1, n // 2 + levels)
    pl.when(inner)(lambda: j_sent(0, levels + 1))
    pl.when(jnp.logical_not(inner))(lambda: j_sent(0, 1))
    x_await(late_place, 2 * late_place, 2, 1)

    @pl.loop(0, chunks)
    def _(block):
        part = x_rows(block)
        x_await(n // 2 + block, 2 * late_place, 2, tall)
        amplitudes(late_place, part)

        @pl.loop(0, depth // wide)
        def _(strip):
            at = pl.ds(pl.multiple_of(strip * wide, wide), wide)
            total[part, at] += jnp.dot(
                amp_parts[part, :], j_parts[:, at], preferred_element_type=jnp.float32
            )

    split_j(last_place, 3)
    x_await(n // 2 + chunks, 2 * last_place, 2, tall)
    amplitudes(last_place, slice(rows - tall, rows))
    drain(x_send.at[pl.ds(0, n - 1), pl.ds(0, rows + 1)], x_send_sem.at[0])


def finish(total_ref, amp_ref, j_ref, out_ref, last_ref, sem):
    rows, depth = total_ref.shape
    tall = last_ref.shape[0]
    ready = rows - tall
    wide = 256

    for start in range(0, ready, tall):
        part = pl.ds(start, tall)
        pltpu.make_async_copy(total_ref.at[part], out_ref.at[part], sem.at[0]).start()
    for start in range(0, depth, wide):
        at = slice(start, start + wide)
        last_ref[:, at] = total_ref[ready:, at] + jnp.dot(
            amp_ref[ready:, :], j_ref[:, at], preferred_element_type=jnp.float32
        )
        pltpu.make_async_copy(
            last_ref.at[:, pl.ds(start, wide)],
            out_ref.at[pl.ds(ready, tall), pl.ds(start, wide)],
            sem.at[0],
        ).start()
    pltpu.make_async_copy(total_ref, out_ref, sem.at[0]).wait()


def fused(i_factors, j_factors, occ_i, occ_j, virt_energy):
    n = lax.axis_size("virt")
    ni, width, depth = i_factors.shape
    nj = j_factors.shape[0]
    rows = ni * width
    anywhere = pl.BlockSpec(memory_space=pl.ANY)
    vmem = pl.BlockSpec(memory_space=pltpu.VMEM)
    f32, bf16 = jnp.float32, jnp.bfloat16
    dma = pltpu.SemaphoreType.DMA
    smem = pltpu.SMEM
    held = pl.pallas_call(
        functools.partial(kernel, n),
        out_shape=(
            pltpu.VMEM((rows, depth), f32),
            pltpu.VMEM((rows, 6 * LANES), bf16),
            pltpu.VMEM((6 * LANES, depth), bf16),
        ),
        in_specs=[anywhere] * 5,
        out_specs=(vmem, vmem, vmem),
        scratch_shapes=[
            pltpu.VMEM((rows, depth), bf16),
            pltpu.VMEM((rows, depth), bf16),
            pltpu.VMEM((n, LANES, depth), f32),
            pltpu.VMEM((n // 2, rows, 2 * LANES), f32),
            pltpu.VMEM((n, rows + 8, LANES), f32),
            pltpu.VMEM((n, rows + 8, LANES), f32),
            pltpu.VMEM((rows, LANES), f32),
            pltpu.VMEM((1, width), f32),
            smem((ni,), f32),
            smem((nj,), f32),
            dma((6,)),
            dma((2,)),
            dma((n + n // 4,)),
            dma((1,)),
            dma((n // 2 + rows // 256 + 1,)),
        ],
        compiler_params=pltpu.CompilerParams(
            collective_id=0, has_side_effects=True, vmem_limit_bytes=50 * 2**20
        ),
        name="pair_exchange",
    )(
        i_factors.reshape(rows, depth), j_factors.reshape(nj * width, depth),
        virt_energy.reshape(1, width), occ_i, occ_j,
    )
    out = pl.pallas_call(
        finish,
        out_shape=jax.ShapeDtypeStruct((rows, depth), f32),
        in_specs=[vmem, vmem, vmem],
        out_specs=anywhere,
        scratch_shapes=[pltpu.VMEM((256, depth), f32), dma((1,))],
        compiler_params=pltpu.CompilerParams(vmem_limit_bytes=4 * 2**20),
        name="store",
    )(*[pltpu.with_memory_space_constraint(array, pltpu.VMEM) for array in held])
    return out.reshape(i_factors.shape)


def transpose_blocks(pair_block, blocks):
    leading = pair_block.shape[:-2]
    height = pair_block.shape[-2]
    width = pair_block.shape[-1]
    parts = pair_block.reshape(leading + (height, blocks, height))
    moved = jnp.swapaxes(parts, -1, -3)
    return moved.reshape(leading + (height, width))


def general(i_factors, j_factors, occ_i, occ_j, virt_energy):
    blocks = lax.axis_size("virt")
    left_rows = i_factors.reshape(-1, i_factors.shape[2])
    density = jnp.zeros(i_factors.shape, jnp.float32)
    whole_energy = lax.all_gather(virt_energy, "virt", axis=0, tiled=True)
    for index in range(j_factors.shape[0]):
        whole_rows = lax.all_gather(j_factors[index], "virt", axis=0, tiled=True)
        pair_block = jnp.dot(left_rows, whole_rows.T, precision=lax.Precision.HIGHEST)
        pair_block = pair_block.reshape(i_factors.shape[0], i_factors.shape[1], whole_rows.shape[0])
        swapped = lax.all_to_all(
            transpose_blocks(pair_block, blocks), "virt", split_axis=2, concat_axis=2, tiled=True
        )
        denominator = (
            virt_energy[None, :, None]
            + whole_energy[None, None, :]
            - occ_i[:, None, None]
            - occ_j[index]
        )
        amplitude = (swapped - 2.0 * pair_block) / denominator
        density = density + jnp.einsum(
            "iab,bp->iap", amplitude, whole_rows, precision=lax.Precision.HIGHEST
        )
    return density


def chip_columns(mesh):
    group = list(mesh.devices.reshape(-1, mesh.shape["virt"])[0])
    if len(group) % 2:
        return 0
    chips = group[::2]
    heights = len({getattr(device, "coords", (0, 0, place))[2] for place, device in enumerate(chips)})
    columns, left = divmod(len(chips), heights)
    return columns if left == 0 and columns in (1, 2) else 0


def body(columns, i_factors, j_factors, occ_i, occ_j, virt_energy):
    ni, width, depth = i_factors.shape
    nj = j_factors.shape[0]
    fits = nj == 2 and nj * width == LANES and (ni * width) % 256 == 0 and depth % 512 == 0
    n = lax.axis_size("virt")
    tall_enough = columns == 2 and n // 4 >= 2
    room = 4 * ni * width * depth * 2 + 4 * n * LANES * (depth + 3 * (ni * width + 8))
    if tall_enough and fits and room < 58 * 2**20:
        return fused(i_factors, j_factors, occ_i, occ_j, virt_energy)
    return general(i_factors, j_factors, occ_i, occ_j, virt_energy)


def solution(mesh):
    placed = (
        P("conf", "virt", None),
        P("conf", "virt", None),
        P("conf"),
        P("conf"),
        P(("conf", "virt")),
    )
    return jax.shard_map(
        functools.partial(body, chip_columns(mesh)),
        mesh=mesh, in_specs=placed, out_specs=P("conf", "virt", None), check_vma=False,
    )
```

```python
import functools

import jax
import jax.numpy as jnp
from jax import lax
from jax.experimental import pallas as pl
from jax.experimental.pallas import tpu as pltpu
from jax.sharding import PartitionSpec as P

LANES = 128
MESH = pl.DeviceIdType.MESH


def split(value):
    high = value.astype(jnp.bfloat16)
    low = (value - high.astype(jnp.float32)).astype(jnp.bfloat16)
    return high, low


def kernel(
    n, i_ref, j_ref, energy_in, occ_i_in, occ_j_in, total, amp_parts, j_parts,
    i_high, i_low, j_all, direct, x_send, x_recv, row_ref, energy_ref, occ_i_ref, occ_j_ref,
    local_sem, j_send_sem, j_recv_sem, x_send_sem, x_recv_sem,
):
    columns = 2
    levels = n // 2 // columns
    me = lax.axis_index("virt")
    core = lax.rem(me, 2)
    chip = me // 2
    y = lax.rem(chip, columns)
    z = chip // columns
    rows, depth = i_ref.shape
    pair = 2 * LANES
    tall = 256
    chunks = rows // tall
    parts = 4
    wide = 512

    load_j = pltpu.make_async_copy(j_ref, j_all.at[me], local_sem.at[1])
    load_j.start()
    load_i = pltpu.make_async_copy(i_ref, total, local_sem.at[0])

    barrier = pltpu.get_barrier_semaphore()

    def greet(device):
        pl.semaphore_signal(barrier, inc=1, device_id={"virt": device}, device_id_type=MESH)

    greet(me + 1 - 2 * core)
    greet(me + 2 * (1 - 2 * y))

    @pl.when(z + 1 < levels)
    def _():
        greet(me + 2 * columns)

    @pl.when(z > 0)
    def _():
        greet(me - 2 * columns)

    inner = jnp.logical_and(z > 0, z + 1 < levels)
    load_i.start()
    small = [
        pltpu.make_async_copy(source, target, local_sem.at[3 + place])
        for place, (source, target) in enumerate(
            ((energy_in, energy_ref), (occ_i_in, occ_i_ref), (occ_j_in, occ_j_ref))
        )
    ]
    for copy in small:
        copy.start()
    pl.semaphore_wait(barrier, 3 + inner.astype(jnp.int32))

    def j_copy(origin, piece, flow, device):
        part = pl.ds(piece * (LANES // parts), LANES // parts)
        ahead = flow == 0 and piece < parts - 1
        slot = n + piece * levels + origin // 2 // columns if ahead else origin
        return pltpu.make_async_remote_copy(
            src_ref=j_all.at[origin, part],
            dst_ref=j_all.at[origin, part],
            send_sem=j_send_sem.at[flow],
            recv_sem=j_recv_sem.at[slot],
            device_id={"virt": device},
            device_id_type=MESH,
        )

    def j_await(origin):
        whole = j_all.at[origin]
        pltpu.make_async_remote_copy(
            src_ref=whole, dst_ref=whole, send_sem=j_send_sem.at[1], recv_sem=j_recv_sem.at[origin],
            device_id={"virt": me}, device_id_type=MESH,
        ).wait_recv()

    def j_send(origin, piece):
        place = origin // 2
        same_core = lax.rem(origin, 2) == core
        in_column = jnp.logical_and(same_core, lax.rem(place, columns) == y)
        from_z = place // columns

        @pl.when(jnp.logical_and(in_column, jnp.logical_and(z >= from_z, z + 1 < levels)))
        def _():
            j_copy(origin, piece, 0, me + 2 * columns).start()

        @pl.when(jnp.logical_and(in_column, jnp.logical_and(z <= from_z, z > 0)))
        def _():
            j_copy(origin, piece, 0, me - 2 * columns).start()

        @pl.when(in_column)
        def _():
            j_copy(origin, piece, 1, me + 2 * (1 - 2 * y)).start()

        @pl.when(same_core)
        def _():
            j_copy(origin, piece, 1, me + 1 - 2 * core).start()

    def drain(sent, sem):
        pltpu.make_async_remote_copy(
            src_ref=sent, dst_ref=sent, send_sem=sem, recv_sem=sem,
            device_id={"virt": me}, device_id_type=MESH,
        ).wait_send()

    def inward(at_z):
        return jnp.where(2 * at_z >= levels, -1, 1)

    def ahead_of(place):
        return place + inward(place // columns) * columns

    def across(place):
        return place + 1 - 2 * lax.rem(place, columns)

    def x_rows(chunk):
        return pl.ds(pl.multiple_of(chunk * tall, tall), tall)

    def x_copy(other, origin, part, slot):
        return pltpu.make_async_remote_copy(
            src_ref=x_send.at[other, part],
            dst_ref=x_recv.at[origin, part],
            send_sem=x_send_sem.at[0],
            recv_sem=x_recv_sem.at[slot],
            device_id={"virt": other},
            device_id_type=MESH,
        )

    def x_block(other, chunk):
        late = across(ahead_of(other // 2)) == chip
        slot = jnp.where(late, n // 2 + core * chunks + chunk, chip)
        return x_copy(other, me, x_rows(chunk), slot)

    def x_held(other, origin):
        return x_copy(
            other, origin, x_rows(chunks - 1), n // 2 + 2 * chunks + lax.rem(origin, 2)
        )

    def x_energy(other):
        return x_copy(other, me, pl.ds(rows, 1), chip)

    def x_await(place, first, sides, count):
        block = x_recv.at[pl.ds(first, sides), pl.ds(0, count)]
        pltpu.make_async_remote_copy(
            src_ref=block, dst_ref=block, send_sem=x_send_sem.at[0], recv_sem=x_recv_sem.at[place],
            device_id={"virt": me}, device_id_type=MESH,
        ).wait_recv()

    def x_stay():
        return pltpu.make_async_copy(x_send.at[me], x_recv.at[me], local_sem.at[2])

    load_j.wait()
    for piece in range(parts):
        j_send(me, piece)
    load_i.wait()

    @pl.loop(0, rows // 32)
    def _(step):
        part = pl.ds(pl.multiple_of(step * 32, 32), 32)
        high, low = split(total[part, :])
        i_high[part, :] = high
        i_low[part, :] = low
        total[part, :] = jnp.zeros((32, depth), jnp.float32)

    for copy in small:
        copy.wait()
    width = energy_ref.shape[1]
    energy = energy_ref[...]
    twice = jnp.concatenate([energy, energy], axis=1)
    tall_energy = jnp.broadcast_to(twice, (LANES, LANES)).T[:width]
    for orbital in range(rows // width):
        row_ref[orbital * width:(orbital + 1) * width, :] = tall_energy - occ_i_ref[orbital]
    col_lane = lax.broadcasted_iota(jnp.int32, (8, LANES), 1)
    col_term = jnp.broadcast_to(twice, (8, LANES)) - jnp.where(
        col_lane < width, occ_j_ref[0], occ_j_ref[1]
    )

    @pl.loop(0, n)
    def _(other):
        x_send[other, pl.ds(rows, 8), :] = col_term

    def split_j(place, copies):
        per = LANES // 32

        @pl.loop(0, 2 * per)
        def _(step):
            from_rows = pl.ds(pl.multiple_of(lax.rem(step, per) * 32, 32), 32)
            high, low = split(j_all[2 * place + step // per, from_rows, :])
            base = pl.multiple_of(step * 32, 32)
            j_parts[pl.ds(base, 32), :] = high
            j_parts[pl.ds(pair + base, 32), :] = low
            if copies == 3:
                j_parts[pl.ds(2 * pair + base, 32), :] = high

    toward = inward(z)
    deepest = jnp.maximum(z, levels - 1 - z)
    beside = 2 * levels
    visits = beside + levels

    def visit(step):
        crossed = step >= beside
        turn = step - beside
        depth_in = jnp.where(turn < deepest - 1, deepest - turn, deepest - 1 - turn)
        depth_in = jnp.where(turn == levels - 1, 1, depth_in)
        distance = step // 2

        def on(way):
            offset = jnp.where(crossed, depth_in, (1 - 2 * way) * distance)
            at_z = z + toward * offset
            valid = jnp.logical_and(at_z >= 0, at_z < levels)
            once = jnp.logical_or(way == 0, jnp.logical_and(step < beside, distance > 0))
            at_y = jnp.where(crossed, columns - 1 - y, y)
            return jnp.logical_and(valid, once), at_z * columns + at_y

        return on, jnp.where(crossed, 0, lax.rem(step, 2))

    @pl.loop(0, visits)
    def _(step):
        on, sign = visit(step)

        @pl.when(sign == 0)
        def _():
            for way in range(2):
                valid, place = on(way)
                origin = 2 * place + core

                @pl.when(jnp.logical_and(jnp.logical_and(valid, step < beside), origin != me))
                def _():
                    for piece in range(parts):
                        j_copy(origin, piece, 0, me).wait_recv()
                        j_send(origin, piece)

            _, place = on(0)
            origin = 2 * place + core

            @pl.when(step >= beside)
            def _():
                j_await(origin)
                for piece in range(parts):
                    j_send(origin, piece)

        valid, place = on(sign)

        @pl.when(valid)
        def _():
            j_await(2 * place + 1 - core)
            for side in range(2):
                other = 2 * place + side

                @pl.when(other != me)
                def _():
                    x_energy(other).start()

            split_j(place, 2)
            lane = lax.broadcasted_iota(jnp.int32, (LANES // 2, LANES), 1)
            half = LANES // 2
            contract = (((1,), (1,)), ((), ()))

            @pl.loop(0, rows // tall)
            def _(block):
                start = pl.multiple_of(block * tall, tall)
                high, low = i_high[pl.ds(start, tall), :], i_low[pl.ds(start, tall), :]
                j_high, j_low = j_parts[pl.ds(0, pair), :], j_parts[pl.ds(pair, pair), :]
                dot = functools.partial(
                    lax.dot_general, dimension_numbers=contract,
                    preferred_element_type=jnp.float32,
                )
                block_pair = dot(high, j_high) + (dot(high, j_low) + dot(low, j_high))
                direct[place, pl.ds(start, tall), :] = block_pair
                for side in range(2):
                    for group in range(tall // LANES):
                        tile = block_pair[
                            group * LANES:(group + 1) * LANES, side * LANES:(side + 1) * LANES
                        ]
                        turned = tile.T
                        moved = pltpu.roll(turned, half, 1)
                        first = jnp.where(lane < half, turned[:half], moved[half:])
                        second = jnp.where(lane < half, moved[:half], turned[half:])
                        base = start + group * LANES
                        x_send[2 * place + side, pl.ds(base, half), :] = first
                        x_send[2 * place + side, pl.ds(base + half, half), :] = second
                hold = jnp.logical_and(ahead_of(place) == chip, block == chunks - 1)
                for side in range(2):
                    other = 2 * place + side

                    @pl.when(jnp.logical_and(other != me, jnp.logical_not(hold)))
                    def _():
                        x_block(other, block).start()

            for side in range(2):
                other = 2 * place + side

                @pl.when(other == me)
                def _():
                    x_stay().start()

    for way in (-1, 1):
        place = chip + way * columns
        there = jnp.logical_and(z + way >= 0, z + way < levels)

        @pl.when(jnp.logical_and(there, ahead_of(place) == chip))
        def _():
            for side in range(2):
                x_held(2 * place + side, me).start()

    last_place = ahead_of(chip)
    late_place = across(last_place)

    def await_place(place):
        @pl.when(place == chip)
        def _():
            x_await(chip, me + 1 - 2 * core, 1, rows + 1)
            x_stay().wait()

        @pl.when(place == last_place)
        def _():
            x_await(place, 2 * place, 2, rows - tall + 1)

        @pl.when(jnp.logical_and(place != chip, place != last_place))
        def _():
            x_await(place, 2 * place, 2, rows + 1)

    def await_late(chunk):
        for side in range(2):
            other = 2 * late_place + side
            x_copy(other, other, x_rows(chunk), n // 2 + side * chunks + chunk).wait_recv()

    def amplitudes(place, part):
        for side in range(2):
            other = 2 * place + side
            lanes = slice(side * LANES, (side + 1) * LANES)
            swapped = x_recv[other, part, :]
            own = direct[place, part, lanes]
            denominator = row_ref[part, :] + x_recv[other, pl.ds(rows, 1), :]
            high, low = split((swapped - 2.0 * own) / denominator)
            amp_parts[part, side * LANES:(side + 1) * LANES] = high
            amp_parts[part, pair + side * LANES:pair + (side + 1) * LANES] = high
            amp_parts[part, 2 * pair + side * LANES:2 * pair + (side + 1) * LANES] = low

    @pl.loop(0, visits)
    def _(step):
        on, sign = visit(step)
        valid, place = on(sign)

        @pl.when(jnp.logical_and(valid, place != late_place))
        def _():
            split_j(place, 3)
            await_place(place)
            arrived = jnp.where(place == last_place, chunks - 1, chunks)

            @pl.loop(0, arrived)
            def _(block):
                amplitudes(place, x_rows(block))

            @pl.when(place == last_place)
            def _():
                amp_parts[rows - tall:, :] = jnp.zeros((tall, 3 * pair), jnp.bfloat16)

            @pl.loop(0, depth // pair)
            def _(strip):
                at = pl.ds(pl.multiple_of(strip * pair, pair), pair)
                total[:, at] += jnp.dot(
                    amp_parts[...], j_parts[:, at], preferred_element_type=jnp.float32
                )

    split_j(late_place, 3)

    def j_sent(flow, blocks):
        drain(j_all.at[pl.ds(0, blocks)], j_send_sem.at[flow])

    j_sent(1, n // 2 + levels)
    pl.when(inner)(lambda: j_sent(0, levels + 1))
    pl.when(jnp.logical_not(inner))(lambda: j_sent(0, 1))
    x_await(late_place, 2 * late_place, 2, 1)

    @pl.loop(0, chunks)
    def _(block):
        part = x_rows(block)
        await_late(block)
        amplitudes(late_place, part)

        @pl.loop(0, depth // wide)
        def _(strip):
            at = pl.ds(pl.multiple_of(strip * wide, wide), wide)
            total[part, at] += jnp.dot(
                amp_parts[part, :], j_parts[:, at], preferred_element_type=jnp.float32
            )

    split_j(last_place, 3)
    for side in range(2):
        x_held(2 * last_place + side, 2 * last_place + side).wait_recv()
    amplitudes(last_place, slice(rows - tall, rows))
    drain(x_send.at[pl.ds(0, n - 1), pl.ds(0, rows + 1)], x_send_sem.at[0])


def finish(total_ref, amp_ref, j_ref, out_ref, last_ref, sems):
    rows, depth = total_ref.shape
    tall = last_ref.shape[0]
    ready = rows // tall - 1
    strips = sems.shape[0] - ready
    wide = depth // strips

    def store(piece):
        part = pl.ds(piece * tall, tall)
        return pltpu.make_async_copy(total_ref.at[part], out_ref.at[part], sems.at[piece])

    def store_last(strip):
        at = pl.ds(strip * wide, wide)
        return pltpu.make_async_copy(
            last_ref.at[:, at], out_ref.at[pl.ds(ready * tall, tall), at], sems.at[ready + strip]
        )

    for piece in range(ready):
        store(piece).start()
    part = slice(ready * tall, rows)
    for strip in range(strips):
        at = slice(strip * wide, (strip + 1) * wide)
        last_ref[:, at] = total_ref[part, at] + jnp.dot(
            amp_ref[part, :], j_ref[:, at], preferred_element_type=jnp.float32
        )
        store_last(strip).start()
    for piece in range(ready):
        store(piece).wait()
    for strip in range(strips):
        store_last(strip).wait()


def fused(i_factors, j_factors, occ_i, occ_j, virt_energy):
    n = lax.axis_size("virt")
    ni, width, depth = i_factors.shape
    nj = j_factors.shape[0]
    rows = ni * width
    anywhere = pl.BlockSpec(memory_space=pl.ANY)
    vmem = pl.BlockSpec(memory_space=pltpu.VMEM)
    f32, bf16 = jnp.float32, jnp.bfloat16
    dma = pltpu.SemaphoreType.DMA
    smem = pltpu.SMEM
    held = pl.pallas_call(
        functools.partial(kernel, n),
        out_shape=(
            pltpu.VMEM((rows, depth), f32),
            pltpu.VMEM((rows, 6 * LANES), bf16),
            pltpu.VMEM((6 * LANES, depth), bf16),
        ),
        in_specs=[anywhere] * 5,
        out_specs=(vmem, vmem, vmem),
        scratch_shapes=[
            pltpu.VMEM((rows, depth), bf16),
            pltpu.VMEM((rows, depth), bf16),
            pltpu.VMEM((n, LANES, depth), f32),
            pltpu.VMEM((n // 2, rows, 2 * LANES), f32),
            pltpu.VMEM((n, rows + 8, LANES), f32),
            pltpu.VMEM((n, rows + 8, LANES), f32),
            pltpu.VMEM((rows, LANES), f32),
            pltpu.VMEM((1, width), f32),
            smem((ni,), f32),
            smem((nj,), f32),
            dma((6,)),
            dma((2,)),
            dma((n + 3 * (n // 4),)),
            dma((1,)),
            dma((n // 2 + 2 * (rows // 256) + 2,)),
        ],
        compiler_params=pltpu.CompilerParams(
            collective_id=0, has_side_effects=True, vmem_limit_bytes=50 * 2**20
        ),
        name="pair_exchange",
    )(
        i_factors.reshape(rows, depth), j_factors.reshape(nj * width, depth),
        virt_energy.reshape(1, width), occ_i, occ_j,
    )
    tall = 256
    strips = 8
    out = pl.pallas_call(
        finish,
        out_shape=jax.ShapeDtypeStruct((rows, depth), f32),
        in_specs=[vmem, vmem, vmem],
        out_specs=anywhere,
        scratch_shapes=[pltpu.VMEM((tall, depth), f32), dma((rows // tall - 1 + strips,))],
        compiler_params=pltpu.CompilerParams(vmem_limit_bytes=4 * 2**20),
        name="store",
    )(*[pltpu.with_memory_space_constraint(array, pltpu.VMEM) for array in held])
    return out.reshape(i_factors.shape)


def transpose_blocks(pair_block, blocks):
    leading = pair_block.shape[:-2]
    height = pair_block.shape[-2]
    width = pair_block.shape[-1]
    parts = pair_block.reshape(leading + (height, blocks, height))
    moved = jnp.swapaxes(parts, -1, -3)
    return moved.reshape(leading + (height, width))


def general(i_factors, j_factors, occ_i, occ_j, virt_energy):
    blocks = lax.axis_size("virt")
    left_rows = i_factors.reshape(-1, i_factors.shape[2])
    density = jnp.zeros(i_factors.shape, jnp.float32)
    whole_energy = lax.all_gather(virt_energy, "virt", axis=0, tiled=True)
    for index in range(j_factors.shape[0]):
        whole_rows = lax.all_gather(j_factors[index], "virt", axis=0, tiled=True)
        pair_block = jnp.dot(left_rows, whole_rows.T, precision=lax.Precision.HIGHEST)
        pair_block = pair_block.reshape(i_factors.shape[0], i_factors.shape[1], whole_rows.shape[0])
        swapped = lax.all_to_all(
            transpose_blocks(pair_block, blocks), "virt", split_axis=2, concat_axis=2, tiled=True
        )
        denominator = (
            virt_energy[None, :, None]
            + whole_energy[None, None, :]
            - occ_i[:, None, None]
            - occ_j[index]
        )
        amplitude = (swapped - 2.0 * pair_block) / denominator
        density = density + jnp.einsum(
            "iab,bp->iap", amplitude, whole_rows, precision=lax.Precision.HIGHEST
        )
    return density


def chip_columns(mesh):
    group = list(mesh.devices.reshape(-1, mesh.shape["virt"])[0])
    if len(group) % 2:
        return 0
    chips = group[::2]
    heights = len({getattr(device, "coords", (0, 0, place))[2] for place, device in enumerate(chips)})
    columns, left = divmod(len(chips), heights)
    return columns if left == 0 and columns in (1, 2) else 0


def body(columns, i_factors, j_factors, occ_i, occ_j, virt_energy):
    ni, width, depth = i_factors.shape
    nj = j_factors.shape[0]
    fits = nj == 2 and nj * width == LANES and (ni * width) % 256 == 0 and depth % 512 == 0
    n = lax.axis_size("virt")
    tall_enough = columns == 2 and n // 4 >= 2
    room = 4 * ni * width * depth * 2 + 4 * n * LANES * (depth + 3 * (ni * width + 8))
    if tall_enough and fits and room < 58 * 2**20:
        return fused(i_factors, j_factors, occ_i, occ_j, virt_energy)
    return general(i_factors, j_factors, occ_i, occ_j, virt_energy)


def solution(mesh):
    placed = (
        P("conf", "virt", None),
        P("conf", "virt", None),
        P("conf"),
        P("conf"),
        P(("conf", "virt")),
    )
    return jax.shard_map(
        functools.partial(body, chip_columns(mesh)),
        mesh=mesh, in_specs=placed, out_specs=P("conf", "virt", None), check_vma=False,
    )
```

```python
import functools

import jax
import jax.numpy as jnp
from jax import lax
from jax.experimental import pallas as pl
from jax.experimental.pallas import tpu as pltpu
from jax.sharding import PartitionSpec as P

LANES = 128
MESH = pl.DeviceIdType.MESH


def split(value):
    high = value.astype(jnp.bfloat16)
    low = (value - high.astype(jnp.float32)).astype(jnp.bfloat16)
    return high, low


def kernel(
    n, i_ref, j_ref, energy_in, occ_i_in, occ_j_in, total, amp_parts, j_parts,
    i_high, i_low, j_all, direct, x_send, x_recv, row_ref, energy_ref, occ_i_ref, occ_j_ref,
    local_sem, j_send_sem, j_recv_sem, x_send_sem, x_recv_sem,
):
    columns = 2
    levels = n // 2 // columns
    me = lax.axis_index("virt")
    core = lax.rem(me, 2)
    chip = me // 2
    y = lax.rem(chip, columns)
    z = chip // columns
    rows, depth = i_ref.shape
    pair = 2 * LANES
    tall = 256
    chunks = rows // tall
    halves = 2
    wide = 512

    load_j = pltpu.make_async_copy(j_ref, j_all.at[me], local_sem.at[1])
    load_j.start()
    load_i = pltpu.make_async_copy(i_ref, total, local_sem.at[0])

    barrier = pltpu.get_barrier_semaphore()

    def greet(device):
        pl.semaphore_signal(barrier, inc=1, device_id={"virt": device}, device_id_type=MESH)

    greet(me + 1 - 2 * core)
    greet(me + 2 * (1 - 2 * y))

    @pl.when(z + 1 < levels)
    def _():
        greet(me + 2 * columns)

    @pl.when(z > 0)
    def _():
        greet(me - 2 * columns)

    inner = jnp.logical_and(z > 0, z + 1 < levels)
    load_i.start()
    small = [
        pltpu.make_async_copy(source, target, local_sem.at[3 + place])
        for place, (source, target) in enumerate(
            ((energy_in, energy_ref), (occ_i_in, occ_i_ref), (occ_j_in, occ_j_ref))
        )
    ]
    for copy in small:
        copy.start()
    pl.semaphore_wait(barrier, 3 + inner.astype(jnp.int32))

    def j_copy(origin, half, flow, device):
        part = pl.ds(half * (LANES // halves), LANES // halves)
        ahead = flow == 0 and half == 0
        slot = n + origin // 2 // columns if ahead else origin
        return pltpu.make_async_remote_copy(
            src_ref=j_all.at[origin, part],
            dst_ref=j_all.at[origin, part],
            send_sem=j_send_sem.at[flow],
            recv_sem=j_recv_sem.at[slot],
            device_id={"virt": device},
            device_id_type=MESH,
        )

    def j_await(origin):
        whole = j_all.at[origin]
        pltpu.make_async_remote_copy(
            src_ref=whole, dst_ref=whole, send_sem=j_send_sem.at[1], recv_sem=j_recv_sem.at[origin],
            device_id={"virt": me}, device_id_type=MESH,
        ).wait_recv()

    def j_send(origin, half):
        place = origin // 2
        same_core = lax.rem(origin, 2) == core
        in_column = jnp.logical_and(same_core, lax.rem(place, columns) == y)
        from_z = place // columns

        @pl.when(jnp.logical_and(in_column, jnp.logical_and(z >= from_z, z + 1 < levels)))
        def _():
            j_copy(origin, half, 0, me + 2 * columns).start()

        @pl.when(jnp.logical_and(in_column, jnp.logical_and(z <= from_z, z > 0)))
        def _():
            j_copy(origin, half, 0, me - 2 * columns).start()

        @pl.when(in_column)
        def _():
            j_copy(origin, half, 1, me + 2 * (1 - 2 * y)).start()

        @pl.when(same_core)
        def _():
            j_copy(origin, half, 1, me + 1 - 2 * core).start()

    def drain(sent, sem):
        pltpu.make_async_remote_copy(
            src_ref=sent, dst_ref=sent, send_sem=sem, recv_sem=sem,
            device_id={"virt": me}, device_id_type=MESH,
        ).wait_send()

    def inward(at_z):
        return jnp.where(2 * at_z >= levels, -1, 1)

    def ahead_of(place):
        return place + inward(place // columns) * columns

    def across(place):
        return place + 1 - 2 * lax.rem(place, columns)

    def x_rows(chunk):
        return pl.ds(pl.multiple_of(chunk * tall, tall), tall)

    def x_copy(other, origin, part, slot):
        return pltpu.make_async_remote_copy(
            src_ref=x_send.at[other, part],
            dst_ref=x_recv.at[origin, part],
            send_sem=x_send_sem.at[0],
            recv_sem=x_recv_sem.at[slot],
            device_id={"virt": other},
            device_id_type=MESH,
        )

    def x_block(other, chunk):
        late = across(ahead_of(other // 2)) == chip
        slot = jnp.where(late, n // 2 + core * chunks + chunk, chip)
        return x_copy(other, me, x_rows(chunk), slot)

    def x_held(other, origin):
        return x_copy(
            other, origin, x_rows(chunks - 1), n // 2 + 2 * chunks + lax.rem(origin, 2)
        )

    def x_energy(other):
        return x_copy(other, me, pl.ds(rows, 1), chip)

    def x_await(place, first, sides, count):
        block = x_recv.at[pl.ds(first, sides), pl.ds(0, count)]
        pltpu.make_async_remote_copy(
            src_ref=block, dst_ref=block, send_sem=x_send_sem.at[0], recv_sem=x_recv_sem.at[place],
            device_id={"virt": me}, device_id_type=MESH,
        ).wait_recv()

    def x_stay():
        return pltpu.make_async_copy(x_send.at[me], x_recv.at[me], local_sem.at[2])

    load_j.wait()
    for half in range(halves):
        j_send(me, half)
    load_i.wait()

    @pl.loop(0, rows // 32)
    def _(step):
        part = pl.ds(pl.multiple_of(step * 32, 32), 32)
        high, low = split(total[part, :])
        i_high[part, :] = high
        i_low[part, :] = low
        total[part, :] = jnp.zeros((32, depth), jnp.float32)

    for copy in small:
        copy.wait()
    width = energy_ref.shape[1]
    energy = energy_ref[...]
    twice = jnp.concatenate([energy, energy], axis=1)
    tall_energy = jnp.broadcast_to(twice, (LANES, LANES)).T[:width]
    for orbital in range(rows // width):
        row_ref[orbital * width:(orbital + 1) * width, :] = tall_energy - occ_i_ref[orbital]
    col_lane = lax.broadcasted_iota(jnp.int32, (8, LANES), 1)
    col_term = jnp.broadcast_to(twice, (8, LANES)) - jnp.where(
        col_lane < width, occ_j_ref[0], occ_j_ref[1]
    )

    @pl.loop(0, n)
    def _(other):
        x_send[other, pl.ds(rows, 8), :] = col_term

    def split_j(place, copies):
        per = LANES // 32

        @pl.loop(0, 2 * per)
        def _(step):
            from_rows = pl.ds(pl.multiple_of(lax.rem(step, per) * 32, 32), 32)
            high, low = split(j_all[2 * place + step // per, from_rows, :])
            base = pl.multiple_of(step * 32, 32)
            j_parts[pl.ds(base, 32), :] = high
            j_parts[pl.ds(pair + base, 32), :] = low
            if copies == 3:
                j_parts[pl.ds(2 * pair + base, 32), :] = high

    toward = inward(z)
    deepest = jnp.maximum(z, levels - 1 - z)
    beside = 2 * levels
    visits = beside + levels

    def visit(step):
        crossed = step >= beside
        turn = step - beside
        depth_in = jnp.where(turn < deepest - 1, deepest - turn, deepest - 1 - turn)
        depth_in = jnp.where(turn == levels - 1, 1, depth_in)
        distance = step // 2

        def on(way):
            offset = jnp.where(crossed, depth_in, (1 - 2 * way) * distance)
            at_z = z + toward * offset
            valid = jnp.logical_and(at_z >= 0, at_z < levels)
            once = jnp.logical_or(way == 0, jnp.logical_and(step < beside, distance > 0))
            at_y = jnp.where(crossed, columns - 1 - y, y)
            return jnp.logical_and(valid, once), at_z * columns + at_y

        return on, jnp.where(crossed, 0, lax.rem(step, 2))

    @pl.loop(0, visits)
    def _(step):
        on, sign = visit(step)

        @pl.when(sign == 0)
        def _():
            for way in range(2):
                valid, place = on(way)
                origin = 2 * place + core

                @pl.when(jnp.logical_and(jnp.logical_and(valid, step < beside), origin != me))
                def _():
                    for half in range(halves):
                        j_copy(origin, half, 0, me).wait_recv()
                        j_send(origin, half)

            _, place = on(0)
            origin = 2 * place + core

            @pl.when(step >= beside)
            def _():
                j_await(origin)
                for half in range(halves):
                    j_send(origin, half)

        valid, place = on(sign)

        @pl.when(valid)
        def _():
            j_await(2 * place + 1 - core)
            for side in range(2):
                other = 2 * place + side

                @pl.when(other != me)
                def _():
                    x_energy(other).start()

            split_j(place, 2)
            lane = lax.broadcasted_iota(jnp.int32, (LANES // 2, LANES), 1)
            half = LANES // 2
            contract = (((1,), (1,)), ((), ()))

            @pl.loop(0, rows // tall)
            def _(block):
                start = pl.multiple_of(block * tall, tall)
                high, low = i_high[pl.ds(start, tall), :], i_low[pl.ds(start, tall), :]
                j_high, j_low = j_parts[pl.ds(0, pair), :], j_parts[pl.ds(pair, pair), :]
                dot = functools.partial(
                    lax.dot_general, dimension_numbers=contract,
                    preferred_element_type=jnp.float32,
                )
                block_pair = dot(high, j_high) + (dot(high, j_low) + dot(low, j_high))
                direct[place, pl.ds(start, tall), :] = block_pair
                for side in range(2):
                    for group in range(tall // LANES):
                        tile = block_pair[
                            group * LANES:(group + 1) * LANES, side * LANES:(side + 1) * LANES
                        ]
                        turned = tile.T
                        moved = pltpu.roll(turned, half, 1)
                        first = jnp.where(lane < half, turned[:half], moved[half:])
                        second = jnp.where(lane < half, moved[:half], turned[half:])
                        base = start + group * LANES
                        x_send[2 * place + side, pl.ds(base, half), :] = first
                        x_send[2 * place + side, pl.ds(base + half, half), :] = second
                hold = jnp.logical_and(ahead_of(place) == chip, block == chunks - 1)
                for side in range(2):
                    other = 2 * place + side

                    @pl.when(jnp.logical_and(other != me, jnp.logical_not(hold)))
                    def _():
                        x_block(other, block).start()

            for side in range(2):
                other = 2 * place + side

                @pl.when(other == me)
                def _():
                    x_stay().start()

    for way in (-1, 1):
        place = chip + way * columns
        there = jnp.logical_and(z + way >= 0, z + way < levels)

        @pl.when(jnp.logical_and(there, ahead_of(place) == chip))
        def _():
            for side in range(2):
                x_held(2 * place + side, me).start()

    last_place = ahead_of(chip)
    late_place = across(last_place)

    def await_place(place):
        @pl.when(place == chip)
        def _():
            x_await(chip, me + 1 - 2 * core, 1, rows + 1)
            x_stay().wait()

        @pl.when(place == last_place)
        def _():
            x_await(place, 2 * place, 2, rows - tall + 1)

        @pl.when(jnp.logical_and(place != chip, place != last_place))
        def _():
            x_await(place, 2 * place, 2, rows + 1)

    def await_late(chunk):
        for side in range(2):
            other = 2 * late_place + side
            x_copy(other, other, x_rows(chunk), n // 2 + side * chunks + chunk).wait_recv()

    def amplitudes(place, part, sides=(0, 1)):
        for side in sides:
            other = 2 * place + side
            lanes = slice(side * LANES, (side + 1) * LANES)
            swapped = x_recv[other, part, :]
            own = direct[place, part, lanes]
            denominator = row_ref[part, :] + x_recv[other, pl.ds(rows, 1), :]
            high, low = split((swapped - 2.0 * own) / denominator)
            amp_parts[part, side * LANES:(side + 1) * LANES] = high
            amp_parts[part, pair + side * LANES:pair + (side + 1) * LANES] = high
            amp_parts[part, 2 * pair + side * LANES:2 * pair + (side + 1) * LANES] = low

    @pl.loop(0, visits)
    def _(step):
        on, sign = visit(step)
        valid, place = on(sign)

        @pl.when(jnp.logical_and(valid, place != late_place))
        def _():
            split_j(place, 3)
            await_place(place)
            arrived = jnp.where(place == last_place, chunks - 1, chunks)

            @pl.loop(0, arrived)
            def _(block):
                amplitudes(place, x_rows(block))

            @pl.when(place == last_place)
            def _():
                amp_parts[rows - tall:, :] = jnp.zeros((tall, 3 * pair), jnp.bfloat16)

            @pl.loop(0, depth // pair)
            def _(strip):
                at = pl.ds(pl.multiple_of(strip * pair, pair), pair)
                total[:, at] += jnp.dot(
                    amp_parts[...], j_parts[:, at], preferred_element_type=jnp.float32
                )

    split_j(late_place, 3)

    def j_sent(flow, blocks):
        drain(j_all.at[pl.ds(0, blocks)], j_send_sem.at[flow])

    j_sent(1, n // 2 + levels)
    pl.when(inner)(lambda: j_sent(0, levels + 1))
    pl.when(jnp.logical_not(inner))(lambda: j_sent(0, 1))
    x_await(late_place, 2 * late_place, 2, 1)

    @pl.loop(0, chunks)
    def _(block):
        part = x_rows(block)
        await_late(block)
        amplitudes(late_place, part)

        @pl.loop(0, depth // wide)
        def _(strip):
            at = pl.ds(pl.multiple_of(strip * wide, wide), wide)
            total[part, at] += jnp.dot(
                amp_parts[part, :], j_parts[:, at], preferred_element_type=jnp.float32
            )

    split_j(last_place, 3)
    for side in range(2):
        x_held(2 * last_place + side, 2 * last_place + side).wait_recv()
        amplitudes(last_place, slice(rows - tall, rows), (side,))
    drain(x_send.at[pl.ds(0, n - 1), pl.ds(0, rows + 1)], x_send_sem.at[0])


def finish(total_ref, amp_ref, j_ref, out_ref, last_ref, sems):
    rows, depth = total_ref.shape
    tall = last_ref.shape[0]
    ready = rows // tall - 1
    strips = sems.shape[0] - ready
    wide = depth // strips

    def store(piece):
        part = pl.ds(piece * tall, tall)
        return pltpu.make_async_copy(total_ref.at[part], out_ref.at[part], sems.at[piece])

    def store_last(strip):
        at = pl.ds(strip * wide, wide)
        return pltpu.make_async_copy(
            last_ref.at[:, at], out_ref.at[pl.ds(ready * tall, tall), at], sems.at[ready + strip]
        )

    for piece in range(ready):
        store(piece).start()
    part = slice(ready * tall, rows)
    for strip in range(strips):
        at = slice(strip * wide, (strip + 1) * wide)
        last_ref[:, at] = total_ref[part, at] + jnp.dot(
            amp_ref[part, :], j_ref[:, at], preferred_element_type=jnp.float32
        )
        store_last(strip).start()
    for piece in range(ready):
        store(piece).wait()
    for strip in range(strips):
        store_last(strip).wait()


def fused(i_factors, j_factors, occ_i, occ_j, virt_energy):
    n = lax.axis_size("virt")
    ni, width, depth = i_factors.shape
    nj = j_factors.shape[0]
    rows = ni * width
    anywhere = pl.BlockSpec(memory_space=pl.ANY)
    vmem = pl.BlockSpec(memory_space=pltpu.VMEM)
    f32, bf16 = jnp.float32, jnp.bfloat16
    dma = pltpu.SemaphoreType.DMA
    smem = pltpu.SMEM
    held = pl.pallas_call(
        functools.partial(kernel, n),
        out_shape=(
            pltpu.VMEM((rows, depth), f32),
            pltpu.VMEM((rows, 6 * LANES), bf16),
            pltpu.VMEM((6 * LANES, depth), bf16),
        ),
        in_specs=[anywhere] * 5,
        out_specs=(vmem, vmem, vmem),
        scratch_shapes=[
            pltpu.VMEM((rows, depth), bf16),
            pltpu.VMEM((rows, depth), bf16),
            pltpu.VMEM((n, LANES, depth), f32),
            pltpu.VMEM((n // 2, rows, 2 * LANES), f32),
            pltpu.VMEM((n, rows + 8, LANES), f32),
            pltpu.VMEM((n, rows + 8, LANES), f32),
            pltpu.VMEM((rows, LANES), f32),
            pltpu.VMEM((1, width), f32),
            smem((ni,), f32),
            smem((nj,), f32),
            dma((6,)),
            dma((2,)),
            dma((n + n // 4,)),
            dma((1,)),
            dma((n // 2 + 2 * (rows // 256) + 2,)),
        ],
        compiler_params=pltpu.CompilerParams(
            collective_id=0, has_side_effects=True, vmem_limit_bytes=50 * 2**20
        ),
        name="pair_exchange",
    )(
        i_factors.reshape(rows, depth), j_factors.reshape(nj * width, depth),
        virt_energy.reshape(1, width), occ_i, occ_j,
    )
    tall = 256
    strips = 4
    out = pl.pallas_call(
        finish,
        out_shape=jax.ShapeDtypeStruct((rows, depth), f32),
        in_specs=[vmem, vmem, vmem],
        out_specs=anywhere,
        scratch_shapes=[pltpu.VMEM((tall, depth), f32), dma((rows // tall - 1 + strips,))],
        compiler_params=pltpu.CompilerParams(vmem_limit_bytes=4 * 2**20),
        name="store",
    )(*[pltpu.with_memory_space_constraint(array, pltpu.VMEM) for array in held])
    return out.reshape(i_factors.shape)


def transpose_blocks(pair_block, blocks):
    leading = pair_block.shape[:-2]
    height = pair_block.shape[-2]
    width = pair_block.shape[-1]
    parts = pair_block.reshape(leading + (height, blocks, height))
    moved = jnp.swapaxes(parts, -1, -3)
    return moved.reshape(leading + (height, width))


def general(i_factors, j_factors, occ_i, occ_j, virt_energy):
    blocks = lax.axis_size("virt")
    left_rows = i_factors.reshape(-1, i_factors.shape[2])
    density = jnp.zeros(i_factors.shape, jnp.float32)
    whole_energy = lax.all_gather(virt_energy, "virt", axis=0, tiled=True)
    for index in range(j_factors.shape[0]):
        whole_rows = lax.all_gather(j_factors[index], "virt", axis=0, tiled=True)
        pair_block = jnp.dot(left_rows, whole_rows.T, precision=lax.Precision.HIGHEST)
        pair_block = pair_block.reshape(i_factors.shape[0], i_factors.shape[1], whole_rows.shape[0])
        swapped = lax.all_to_all(
            transpose_blocks(pair_block, blocks), "virt", split_axis=2, concat_axis=2, tiled=True
        )
        denominator = (
            virt_energy[None, :, None]
            + whole_energy[None, None, :]
            - occ_i[:, None, None]
            - occ_j[index]
        )
        amplitude = (swapped - 2.0 * pair_block) / denominator
        density = density + jnp.einsum(
            "iab,bp->iap", amplitude, whole_rows, precision=lax.Precision.HIGHEST
        )
    return density


def chip_columns(mesh):
    group = list(mesh.devices.reshape(-1, mesh.shape["virt"])[0])
    if len(group) % 2:
        return 0
    chips = group[::2]
    heights = len({getattr(device, "coords", (0, 0, place))[2] for place, device in enumerate(chips)})
    columns, left = divmod(len(chips), heights)
    return columns if left == 0 and columns in (1, 2) else 0


def body(columns, i_factors, j_factors, occ_i, occ_j, virt_energy):
    ni, width, depth = i_factors.shape
    nj = j_factors.shape[0]
    fits = nj == 2 and nj * width == LANES and (ni * width) % 256 == 0 and depth % 512 == 0
    n = lax.axis_size("virt")
    tall_enough = columns == 2 and n // 4 >= 2
    room = 4 * ni * width * depth * 2 + 4 * n * LANES * (depth + 3 * (ni * width + 8))
    if tall_enough and fits and room < 58 * 2**20:
        return fused(i_factors, j_factors, occ_i, occ_j, virt_energy)
    return general(i_factors, j_factors, occ_i, occ_j, virt_energy)


def solution(mesh):
    placed = (
        P("conf", "virt", None),
        P("conf", "virt", None),
        P("conf"),
        P("conf"),
        P(("conf", "virt")),
    )
    return jax.shard_map(
        functools.partial(body, chip_columns(mesh)),
        mesh=mesh, in_specs=placed, out_specs=P("conf", "virt", None), check_vma=False,
    )
```
